512 devices in a mesh: grp: 32 (over y, z_hi), chan: 16 (over z_lo, x, core).
Axes of the slice: x: 4, y: 8, z: 8 (z_hi: 4, z_lo: 2; z = z_hi * 2 + z_lo), core: 2. Of those that a mesh axis runs over, the one named last changes fastest.
Arguments:
- grad_out: bfloat16 [256, 32, 16, 128], P('grp', 'chan'), may hold values from -6 to 6
- feat_full: bfloat16 [256, 32, 16, 128], P('grp', 'chan'), may hold values from -6 to 6
- filters_full: bfloat16 [3, 3, 3, 128, 128], replicated, may hold values from -0.109375 to 0.109375
- upsample_weight: bfloat16 [2, 2, 2, 512, 128], replicated, may hold values from -0.1875 to 0.1875
- filters_half: bfloat16 [3, 3, 3, 512, 512], P(None, None, None, None, 'chan'), may hold values from -0.0546875 to 0.0546875
Outputs:
- grad_half: bfloat16 [16, 128, 8, 512], P('chan', 'grp')
- taps_grad: float32 [3, 3, 3, 128, 128], P(None, None, None, 'grp', 'chan')
The draws below stay inside these ranges and needn't reach their ends.
All inputs are finite; a program needn't handle non-finite values.
Results may differ from the reference program's by a relative error of at most 0.0058.
Values may be sent and summed in bfloat16 or wider, within the bound.
A program may use at most 64 MiB of HBM per device.

```python
import jax
import jax.numpy as jnp
from jax import lax

HALF_CH = 512
FULL_CH = 128
NX = 256
NY = 32
NZ = 16


def steps_of(stream_key, shape, pieces, least, high):
    factor_of, own = 1.0, jax.random.fold_in(stream_key, 6)
    for axis_at, shards_of in pieces:
        heights = jnp.exp(jax.random.uniform(jax.random.fold_in(own, axis_at), (shards_of,), jnp.float32, least / len(pieces), high / len(pieces)))
        factor_of = factor_of * jnp.repeat(heights, shape[axis_at] // shards_of).reshape([-1 if axis == axis_at else 1 for axis in range(len(shape))])
    return factor_of


def normal_values(own_key, dims, deviation, most, pieces=(), kind=jnp.bfloat16):
    drawn = jax.random.normal(own_key, dims, jnp.float32) * deviation
    if len(pieces) > 0:
        drawn = steps_of(own_key, dims, pieces, -0.22, 0.18) * drawn
    return jnp.clip(drawn, min=-most, max=most).astype(kind)


def setup_inputs(seed: int = 0) -> dict:
    streams_of = jax.random.split(jax.random.key(seed), 6)
    grad_out = normal_values(streams_of[0], (NX, NY, NZ, FULL_CH), 1.0, 6.0, ((0, 32), (1, 16)))
    feat_full = normal_values(streams_of[1], (NX, NY, NZ, FULL_CH), 1.0, 6.0, ((0, 32), (1, 16)))
    filters_full = normal_values(streams_of[2], (3, 3, 3, FULL_CH, FULL_CH), (27 * FULL_CH) ** -0.5, 0.109375)
    upsample_weight = normal_values(streams_of[3], (2, 2, 2, HALF_CH, FULL_CH), (8 * FULL_CH) ** -0.5, 0.1875)
    filters_half = normal_values(streams_of[4], (3, 3, 3, HALF_CH, HALF_CH), (27 * HALF_CH) ** -0.5, 0.0546875, ((4, 16),))
    return dict(grad_out=grad_out, feat_full=feat_full, filters_full=filters_full, upsample_weight=upsample_weight, filters_half=filters_half)


def conv_transpose(field, weight):
    extent = field.shape[:3]
    padded = jnp.pad(field, ((1, 1), (1, 1), (1, 1), (0, 0)))
    summed = jnp.zeros(extent + (weight.shape[3],), jnp.float32)
    for p in range(3):
        for q in range(3):
            for r in range(3):
                window = padded[2 - p:2 - p + extent[0], 2 - q:2 - q + extent[1], 2 - r:2 - r + extent[2]]
                summed = summed + jnp.einsum("xyzo,io->xyzi", window, weight[p, q, r], precision=lax.Precision.HIGHEST)
    return summed


def reference(grad_out, feat_full, filters_full, upsample_weight, filters_half):
    upward = grad_out.astype(jnp.float32)
    features = feat_full.astype(jnp.float32)
    extent = grad_out.shape[:3]
    channels = grad_out.shape[3]
    input_grad = conv_transpose(upward, filters_full.astype(jnp.float32)).astype(jnp.bfloat16)
    padded = jnp.pad(features, ((1, 1), (1, 1), (1, 1), (0, 0)))
    tap_list = []
    for p in range(3):
        for q in range(3):
            for r in range(3):
                window = padded[p:p + extent[0], q:q + extent[1], r:r + extent[2]]
                tap_list.append(jnp.einsum("xyzi,xyzo->io", window, upward, precision=lax.Precision.HIGHEST))
    taps_grad = jnp.stack(tap_list).reshape(3, 3, 3, channels, channels)
    halves = input_grad.astype(jnp.float32).reshape(extent[0] // 2, 2, extent[1] // 2, 2, extent[2] // 2, 2, channels)
    coarse = jnp.einsum("iajbkcd,abced->jike", halves, upsample_weight.astype(jnp.float32), precision=lax.Precision.HIGHEST).astype(jnp.bfloat16)
    swapped = jnp.transpose(filters_half.astype(jnp.float32), (1, 0, 2, 3, 4))
    grad_half = conv_transpose(coarse.astype(jnp.float32), swapped).astype(jnp.bfloat16)
    return grad_half, taps_grad
```

```python
import jax
import jax.numpy as jnp
from jax import lax
from jax.experimental import pallas as pl
from jax.experimental.pallas import tpu as pltpu
from jax.sharding import PartitionSpec as P

F32 = jnp.float32
BF16 = jnp.bfloat16
MESH = pl.DeviceIdType.MESH
NT = (((1,), (1,)), ((), ()))
TN = (((0,), (0,)), ((), ()))
ZHI = 4


def kernel(
    go, fe, wf, uw, wh,
    gh_out, tg_out,
    G, FE, WF, UP, WP, IG,
    T, XS, XR, SS, SR,
    PS, PR, SA, FS, FR,
    VT, YS, YR, ZS, ZR,
    lsem, hs, hr, ws, wr, xs, xr, ss, sr, ps, pr, fs, fr, ys, yr, zs, zr,
):
    g = lax.axis_index("grp")
    c = lax.axis_index("chan")
    ngrp = lax.axis_size("grp")
    nchan = lax.axis_size("chan")
    nchip = nchan // 2
    ny = ngrp // ZHI
    y, zh = g // ZHI, lax.rem(g, ZHI)
    chip, core = c // 2, lax.rem(c, 2)

    def dev(gi, ci):
        return {"grp": gi, "chan": ci}

    def remote(src, dst, send, recv, gi, ci):
        return pltpu.make_async_remote_copy(
            src_ref=src, dst_ref=dst, send_sem=send, recv_sem=recv,
            device_id=dev(gi, ci), device_id_type=MESH,
        )

    def group_of(s):
        return lax.rem(c + s, nchan)

    def ygrp(s):
        return lax.rem(y + s, ny) * ZHI + zh

    def zgrp(s):
        return y * ZHI + lax.rem(zh + s, ZHI)

    l_go = pltpu.make_async_copy(go, G.at[3:11, 1:3], lsem.at[0])
    l_wh = [
        pltpu.make_async_copy(
            wh.at[t], WP.at[:, :, pl.ds(pl.multiple_of(t * 64 + core * 32, 32), 32), :], lsem.at[1 + t]
        )
        for t in range(3)
    ]
    l_fe = pltpu.make_async_copy(fe, FE, lsem.at[4])
    l_wf = pltpu.make_async_copy(wf, WF, lsem.at[5])
    l_up = pltpu.make_async_copy(uw, UP, lsem.at[6])
    l_go.start()
    l_fe.start()
    for t in range(3):
        l_wh[t].start()
    l_wf.start()
    l_up.start()

    barrier = pltpu.get_barrier_semaphore()

    def hello(gi, ci):
        pl.semaphore_signal(barrier, inc=1, device_id=dev(gi, ci), device_id_type=MESH)

    def hello_group(s, _):
        hello(g, group_of(s))
        return 0

    def hello_y(s, _):
        hello(ygrp(s), c)
        return 0

    def hello_z(s, _):
        hello(zgrp(s), c)
        return 0

    for dg in (1, ngrp - 1):
        for dc in (0, 1, nchan - 1):
            hello(lax.rem(g + dg, ngrp), group_of(dc))
    lax.fori_loop(1, nchan, hello_group, 0)
    lax.fori_loop(1, ny, hello_y, 0)
    lax.fori_loop(1, ZHI, hello_z, 0)

    PR[0] = jnp.zeros(PR.shape[1:], BF16)
    PR[nchan + 1] = jnp.zeros(PR.shape[1:], BF16)
    WP[:, :, 192:256, :] = jnp.zeros((3, 3, 64, WP.shape[3]), BF16)
    T[:, :, 216:224, :] = jnp.zeros((2, nchip, 8, 128), F32)
    l_fe.wait()
    feat = FE[...].reshape(256, 128).astype(F32)
    z_of = lax.broadcasted_iota(jnp.int32, (256, 128), 0) % 16
    before = jnp.where(z_of > 0, pltpu.roll(feat, 1, 0), 0.0)
    after = jnp.where(z_of < 15, pltpu.roll(feat, 255, 0), 0.0)
    feat3 = jnp.concatenate([before, feat, after], axis=1).astype(BF16)
    l_go.wait()

    pl.semaphore_wait(barrier, (nchan - 1) + (ny - 1) + (ZHI - 1) + 6)

    xsrc = {0: (3, 11), 1: (8, 11), 2: (3, 6)}
    xdst = {0: (3, 11), 1: (0, 3), 2: (11, 14)}
    ysrc = {0: (1, 3), 1: (2, 3), 2: (1, 2)}
    ydst = {0: (1, 3), 1: (0, 1), 2: (3, 4)}
    gstep = {0: 0, 1: 1, 2: ngrp - 1}
    cstep = {0: 0, 1: 1, 2: nchan - 1}
    halos = []
    for a, b in ((1, 0), (2, 0), (1, 1), (1, 2), (2, 1), (2, 2), (0, 1), (0, 2)):
        halos.append(
            remote(
                G.at[xsrc[a][0]:xsrc[a][1], ysrc[b][0]:ysrc[b][1]],
                G.at[xdst[a][0]:xdst[a][1], ydst[b][0]:ydst[b][1]],
                hs.at[a * 3 + b], hr.at[a * 3 + b],
                lax.rem(g + gstep[a], ngrp), group_of(cstep[b]),
            )
        )
    for h in halos:
        h.start()
    other = c + 1 - 2 * core
    wcopies = []
    for t in range(3):
        l_wh[t].wait()
        rows = WP.at[:, :, pl.ds(pl.multiple_of(t * 64 + core * 32, 32), 32), :]
        wcopies.append(remote(rows, rows, ws.at[t], wr.at[t], g, other))
        wcopies[-1].start()
    l_wf.wait()
    l_up.wait()
    for h in halos:
        h.wait_recv()

    @pl.when(g == 0)
    def _():
        G[0:3] = jnp.zeros((3,) + G.shape[1:], BF16)

    @pl.when(g == ngrp - 1)
    def _():
        G[11:14] = jnp.zeros((3,) + G.shape[1:], BF16)

    @pl.when(c == 0)
    def _():
        G[:, 0:1] = jnp.zeros((14, 1, 16, 128), BF16)

    @pl.when(c == nchan - 1)
    def _():
        G[:, 3:4] = jnp.zeros((14, 1, 16, 128), BF16)

    for tx in range(3):
        window = jnp.concatenate(
            [G[4 - tx:12 - tx, 2 - ty:4 - ty].reshape(256, 128) for ty in range(3)], axis=1
        )
        part = lax.dot_general(window, feat3, TN, preferred_element_type=F32)
        for ty in range(3):
            rows = part[ty * 128:(ty + 1) * 128].reshape(nchip, 2, 8, 384)
            for tz in range(3):
                at = ((tx * 3 + ty) * 3 + tz) * 8
                for k in range(2):
                    T[k, :, at:at + 8, :] = rows[:, k, :, tz * 128:(tz + 1) * 128]
    XS[...] = T[1 - core].astype(BF16)
    xcopy = remote(XS, XR, xs, xr, g, other)
    xcopy.start()

    lhs = jnp.concatenate(
        [
            G[2 - tx:14 - tx, 2 - ty:4 - ty].reshape(384, 128)
            for tx in range(3)
            for ty in range(3)
        ],
        axis=1,
    )
    rhs = jnp.concatenate(
        [WF[tx, ty].reshape(384, 128) for tx in range(3) for ty in range(3)], axis=1
    )
    grown = lax.dot_general(lhs, rhs, NT, preferred_element_type=F32)
    z_at = lax.broadcasted_iota(jnp.int32, (384, 128), 0) % 16
    up = jnp.where(z_at < 15, pltpu.roll(grown[:, 0:128], 383, 0), 0.0)
    down = jnp.where(z_at > 0, pltpu.roll(grown[:, 256:384], 1, 0), 0.0)
    IG[...] = grown[:, 128:256] + up + down

    coarse = jnp.zeros((48, 512), F32)
    for a in range(2):
        for b in range(2):
            cells = jnp.concatenate(
                [
                    jnp.concatenate(
                        [IG[pl.ds(((2 * i + a) * 2 + b) * 16 + k, 8, stride=2), :] for i in range(6)],
                        axis=0,
                    )
                    for k in range(2)
                ],
                axis=1,
            ).astype(BF16)
            weight = jnp.concatenate([UP[a, b, 0], UP[a, b, 1]], axis=1)
            coarse = coarse + lax.dot_general(cells, weight, NT, preferred_element_type=F32)
    row_of = lax.broadcasted_iota(jnp.int32, (48, 512), 0)
    outside = ((row_of < 8) & (g == 0)) | ((row_of >= 40) & (g == ngrp - 1))
    coarse = jnp.where(outside, 0.0, coarse)
    low = lax.broadcasted_iota(jnp.int32, (8, 128), 1) < 64
    for q in range(4):
        block = coarse[:, q * 128:(q + 1) * 128]
        turned = pltpu.roll(block, 64, 1)
        for half in range(2):
            same, swap = (block, turned) if half == 0 else (turned, block)
            d = 2 * q + half
            for k in range(2):
                pair = []
                for i in (2 * k, 2 * k + 1):
                    s0, s1, s2 = (i + 2) * 8, (i + 1) * 8, i * 8
                    first = jnp.where(low, same[s0:s0 + 8], swap[s1:s1 + 8])
                    pair.append(jnp.concatenate([first, same[s2:s2 + 8]], axis=1))
                PS[2 * d + k] = jnp.concatenate(pair, axis=0).astype(BF16)

    def pcopy(s):
        d = group_of(s)
        return remote(PS.at[d], PR.at[c + 1], ps.at[d], pr.at[c], g, d)

    def psend(s, _):
        pcopy(s).start()
        return 0

    lax.fori_loop(1, nchan, psend, 0)
    PR[c + 1] = PS[c]

    xcopy.wait_recv()
    T[core] = T[core] + XR[...].astype(F32)
    SS[...] = T[core].astype(BF16)

    def scopy(s):
        d = lax.rem(chip + s, nchip)
        return remote(SS.at[d], SR.at[chip], ss.at[d], sr.at[chip], g, 2 * d + core)

    def ssend(s, _):
        scopy(s).start()
        return 0

    lax.fori_loop(1, nchip, ssend, 0)

    for w in wcopies:
        w.wait_recv()

    def precv(s, _):
        o = group_of(s)
        remote(PS.at[o], PR.at[o + 1], ps.at[o], pr.at[o], g, o).wait_recv()
        return 0

    lax.fori_loop(1, nchan, precv, 0)
    rows = (nchan + 2) * 16
    slab = PR[...].reshape(rows, 256).astype(F32)
    k_of = lax.broadcasted_iota(jnp.int32, (rows, 256), 0) % 8
    SA[0] = jnp.where(k_of < 7, pltpu.roll(slab, rows - 1, 0), 0.0).astype(BF16).reshape(SA.shape[1:])
    SA[1] = PR[...]
    SA[2] = jnp.where(k_of > 0, pltpu.roll(slab, 1, 0), 0.0).astype(BF16).reshape(SA.shape[1:])
    lhs = jnp.concatenate(
        [
            SA[tz, 2 - ty:2 - ty + nchan].reshape(nchan * 16, 256)
            for ty in range(3)
            for tz in range(3)
        ],
        axis=1,
    )
    part = jnp.dot(lhs, WP[...].reshape(9 * 256, 512), preferred_element_type=F32)
    FS[...] = part.astype(BF16).reshape(FS.shape)

    def fcopy(s):
        d = group_of(s)
        return remote(FS.at[d], FR.at[c], fs.at[d], fr.at[c], g, d)

    def fsend(s, _):
        fcopy(s).start()
        return 0

    lax.fori_loop(1, nchan, fsend, 0)
    FR[c] = FS[c]

    total = T[core, chip]

    def srecv(s, acc):
        o = lax.rem(chip + s, nchip)
        remote(SS.at[o], SR.at[o], ss.at[o], sr.at[o], g, 2 * o + core).wait_recv()
        return acc + SR[o].astype(F32)

    total = lax.fori_loop(1, nchip, srecv, total)
    flipped = jnp.concatenate([total, jnp.zeros((32, 128), F32)], axis=0).T
    VT[...] = flipped.reshape(VT.shape)
    YS[...] = flipped.astype(BF16).reshape(YS.shape)

    def ycopy(s):
        d = lax.rem(y + s, ny)
        return remote(YS.at[d], YR.at[y], ys.at[d], yr.at[y], d * ZHI + zh, c)

    def ysend(s, _):
        ycopy(s).start()
        return 0

    lax.fori_loop(1, ny, ysend, 0)

    def frecv(s, _):
        o = group_of(s)
        remote(FS.at[o], FR.at[o], fs.at[o], fr.at[o], g, o).wait_recv()
        return 0

    lax.fori_loop(1, nchan, frecv, 0)
    for k in range(2):
        acc = FR[k].astype(F32)
        for p in range(1, nchan // 2):
            acc = acc + FR[2 * p + k].astype(F32)
        gh_out[k * 16:(k + 1) * 16, :] = acc.astype(BF16)

    def yrecv(s, acc):
        o = lax.rem(y + s, ny)
        remote(YS.at[o], YR.at[o], ys.at[o], yr.at[o], o * ZHI + zh, c).wait_recv()
        return acc + YR[o].astype(F32)

    v2 = lax.fori_loop(1, ny, yrecv, VT[y])
    for q in range(ZHI):
        ZS[q] = jnp.concatenate([v2[4 * q:4 * q + 4], jnp.zeros((4, 256), F32)], axis=0)

    def zcopy(s):
        d = lax.rem(zh + s, ZHI)
        return remote(ZS.at[d], ZR.at[zh], zs.at[d], zr.at[zh], y * ZHI + d, c)

    def zsend(s, _):
        zcopy(s).start()
        return 0

    lax.fori_loop(1, ZHI, zsend, 0)

    def zrecv(s, acc):
        o = lax.rem(zh + s, ZHI)
        remote(ZS.at[o], ZR.at[o], zs.at[o], zr.at[o], y * ZHI + o, c).wait_recv()
        return acc + ZR[o]

    v3 = lax.fori_loop(1, ZHI, zrecv, ZS[zh])
    for t in range(27):
        tg_out[t] = v3[0:4, 8 * t:8 * t + 8]

    for h in halos:
        h.wait_send()
    for w in wcopies:
        w.wait_send()
    xcopy.wait_send()

    def sent_group(s, _):
        pcopy(s).wait_send()
        fcopy(s).wait_send()
        return 0

    def sent_chip(s, _):
        scopy(s).wait_send()
        return 0

    def sent_y(s, _):
        ycopy(s).wait_send()
        return 0

    def sent_z(s, _):
        zcopy(s).wait_send()
        return 0

    lax.fori_loop(1, nchan, sent_group, 0)
    lax.fori_loop(1, nchip, sent_chip, 0)
    lax.fori_loop(1, ny, sent_y, 0)
    lax.fori_loop(1, ZHI, sent_z, 0)


def body(grad_out, feat_full, filters_full, upsample_weight, filters_half):
    nchan = lax.axis_size("chan")
    ny = lax.axis_size("grp") // ZHI
    nchip = nchan // 2
    wide = filters_half.shape[3]
    turned = jnp.swapaxes(filters_half, 3, 4)
    V = pltpu.VMEM
    D = pltpu.SemaphoreType.DMA
    anyspace = pl.BlockSpec(memory_space=pl.ANY)
    vmem = pl.BlockSpec(memory_space=pltpu.VMEM)
    grad_half, taps = pl.pallas_call(
        kernel,
        out_shape=(
            jax.ShapeDtypeStruct((32, wide), BF16),
            jax.ShapeDtypeStruct((27, 4, 8), F32),
        ),
        in_specs=[anyspace] * 5,
        out_specs=(vmem, vmem),
        scratch_shapes=[
            V((14, 4, 16, 128), BF16),
            V((8, 2, 16, 128), BF16),
            V((3, 3, 3, 128, 128), BF16),
            V((2, 2, 2, wide, 128), BF16),
            V((3, 3, 256, wide), BF16),
            V((384, 128), F32),
            V((2, nchip, 224, 128), F32),
            V((nchip, 224, 128), BF16),
            V((nchip, 224, 128), BF16),
            V((nchip, 224, 128), BF16),
            V((nchip, 224, 128), BF16),
            V((nchan, 16, 256), BF16),
            V((nchan + 2, 16, 256), BF16),
            V((3, nchan + 2, 16, 256), BF16),
            V((nchan, 16, wide), BF16),
            V((nchan, 16, wide), BF16),
            V((ny, 16, 256), F32),
            V((ny, 16, 256), BF16),
            V((ny, 16, 256), BF16),
            V((ZHI, 8, 256), F32),
            V((ZHI, 8, 256), F32),
            D((7,)),
            D((9,)), D((9,)),
            D((3,)), D((3,)),
            D, D,
            D((nchip,)), D((nchip,)),
            D((nchan,)), D((nchan,)),
            D((nchan,)), D((nchan,)),
            D((ny,)), D((ny,)),
            D((ZHI,)), D((ZHI,)),
        ],
        compiler_params=pltpu.CompilerParams(collective_id=0, has_side_effects=True),
    )(grad_out, feat_full, filters_full, upsample_weight, turned)
    return grad_half.reshape(1, 4, 8, wide), taps.reshape(3, 3, 3, 4, 8)


def solution(mesh):
    in_specs = (
        P("grp", "chan", None, None),
        P("grp", "chan", None, None),
        P(),
        P(),
        P(None, None, None, None, "chan"),
    )
    out_specs = (P("chan", "grp", None, None), P(None, None, None, "grp", "chan"))
    return jax.shard_map(body, mesh=mesh, in_specs=in_specs, out_specs=out_specs, check_vma=False)
```

```python
import jax
import jax.numpy as jnp
from jax import lax
from jax.experimental import pallas as pl
from jax.experimental.pallas import tpu as pltpu
from jax.sharding import PartitionSpec as P

F32 = jnp.float32
BF16 = jnp.bfloat16
MESH = pl.DeviceIdType.MESH
NT = (((1,), (1,)), ((), ()))
TN = (((0,), (0,)), ((), ()))
ZHI = 4


def kernel(
    go, fe, wf, uw, wh,
    gh_out, tg_out,
    G, FE, WF, UP, WP, IG,
    T, XS, XR, SS, SR,
    PS, PR, SA, FS, FR,
    VT, YS, YR, ZS, ZR,
    lsem, hs, hr, hs2, hr2, ws, wr, xs, xr, ss, sr, ps, pr, fs, fr, ys, yr, zs, zr,
):
    g = lax.axis_index("grp")
    c = lax.axis_index("chan")
    ngrp = lax.axis_size("grp")
    nchan = lax.axis_size("chan")
    nchip = nchan // 2
    ny = ngrp // ZHI
    y, zh = g // ZHI, lax.rem(g, ZHI)
    chip, core = c // 2, lax.rem(c, 2)

    def dev(gi, ci):
        return {"grp": gi, "chan": ci}

    def remote(src, dst, send, recv, gi, ci):
        return pltpu.make_async_remote_copy(
            src_ref=src, dst_ref=dst, send_sem=send, recv_sem=recv,
            device_id=dev(gi, ci), device_id_type=MESH,
        )

    def group_of(s):
        return lax.rem(c + s, nchan)

    def ygrp(s):
        return lax.rem(y + s, ny) * ZHI + zh

    def zgrp(s):
        return y * ZHI + lax.rem(zh + s, ZHI)

    def ycopy(s, part):
        d = lax.rem(y + s, ny)
        return remote(
            YS.at[part, d], YR.at[part, y], ys.at[part, d], yr.at[part, y], d * ZHI + zh, c
        )

    l_go = pltpu.make_async_copy(go, G.at[3:11, 1:3], lsem.at[0])
    l_wh = [
        pltpu.make_async_copy(
            wh.at[t], WP.at[:, :, pl.ds(pl.multiple_of(t * 64 + core * 32, 32), 32), :], lsem.at[1 + t]
        )
        for t in range(3)
    ]
    l_fe = pltpu.make_async_copy(fe, FE, lsem.at[4])
    l_wf = pltpu.make_async_copy(wf, WF, lsem.at[5])
    l_up = pltpu.make_async_copy(uw, UP, lsem.at[6])
    l_go.start()
    l_fe.start()
    for t in range(3):
        l_wh[t].start()
    l_wf.start()
    l_up.start()

    barrier = pltpu.get_barrier_semaphore()

    def hello(gi, ci):
        pl.semaphore_signal(barrier, inc=1, device_id=dev(gi, ci), device_id_type=MESH)

    def hello_group(s, _):
        hello(g, group_of(s))
        return 0

    def hello_y(s, _):
        hello(ygrp(s), c)
        return 0

    def hello_z(s, _):
        hello(zgrp(s), c)
        return 0

    for dg in (1, ngrp - 1):
        for dc in (1, nchan - 1, 0):
            hello(lax.rem(g + dg, ngrp), group_of(dc))
    lax.fori_loop(1, ny, hello_y, 0)
    lax.fori_loop(1, ZHI, hello_z, 0)
    lax.fori_loop(1, nchan, hello_group, 0)

    PR[0] = jnp.zeros(PR.shape[1:], BF16)
    PR[nchan + 1] = jnp.zeros(PR.shape[1:], BF16)
    WP[:, :, 192:256, :] = jnp.zeros((3, 3, 64, WP.shape[3]), BF16)
    T[:, :, 216:224, :] = jnp.zeros((2, nchip, 8, 128), F32)
    l_fe.wait()
    feat = FE[...].reshape(256, 128).astype(F32)
    z_of = lax.broadcasted_iota(jnp.int32, (256, 128), 0) % 16
    before = jnp.where(z_of > 0, pltpu.roll(feat, 1, 0), 0.0)
    after = jnp.where(z_of < 15, pltpu.roll(feat, 255, 0), 0.0)
    feat3 = jnp.concatenate([before, feat, after], axis=1).astype(BF16)
    l_go.wait()

    pl.semaphore_wait(barrier, (nchan - 1) + (ny - 1) + (ZHI - 1) + 6)

    ysrc = {0: (1, 3), 1: (2, 3), 2: (1, 2)}
    ydst = {0: (1, 3), 1: (0, 1), 2: (3, 4)}
    gstep = {0: 0, 1: 1, 2: ngrp - 1}
    cstep = {0: 0, 1: 1, 2: nchan - 1}

    def halo(a, b, src, dst, send, recv):
        return remote(
            G.at[src[0]:src[1], ysrc[b][0]:ysrc[b][1]],
            G.at[dst[0]:dst[1], ydst[b][0]:ydst[b][1]],
            send.at[a * 3 + b], recv.at[a * 3 + b],
            lax.rem(g + gstep[a], ngrp), group_of(cstep[b]),
        )

    near_src = {0: (3, 11), 1: (10, 11), 2: (3, 4)}
    near_dst = {0: (3, 11), 1: (2, 3), 2: (11, 12)}
    far_src = {1: (8, 10), 2: (4, 6)}
    far_dst = {1: (0, 2), 2: (12, 14)}
    near = [
        halo(a, b, near_src[a], near_dst[a], hs, hr)
        for a, b in ((1, 1), (1, 2), (2, 1), (2, 2), (1, 0), (2, 0), (0, 1), (0, 2))
    ]
    far = [
        halo(a, b, far_src[a], far_dst[a], hs2, hr2)
        for a, b in ((1, 1), (1, 2), (2, 1), (2, 2), (1, 0), (2, 0))
    ]
    for h in near:
        h.start()
    for h in far:
        h.start()
    other = c + 1 - 2 * core
    wcopies = []
    for t in range(3):
        l_wh[t].wait()
        rows = WP.at[:, :, pl.ds(pl.multiple_of(t * 64 + core * 32, 32), 32), :]
        wcopies.append(remote(rows, rows, ws.at[t], wr.at[t], g, other))
        wcopies[-1].start()
    for h in near:
        h.wait_recv()

    @pl.when(g == 0)
    def _():
        G[2:3] = jnp.zeros((1,) + G.shape[1:], BF16)

    @pl.when(g == ngrp - 1)
    def _():
        G[11:12] = jnp.zeros((1,) + G.shape[1:], BF16)

    @pl.when(c == 0)
    def _():
        G[2:12, 0:1] = jnp.zeros((10, 1, 16, 128), BF16)

    @pl.when(c == nchan - 1)
    def _():
        G[2:12, 3:4] = jnp.zeros((10, 1, 16, 128), BF16)

    xcopies = []
    for tx in range(3):
        window = jnp.concatenate(
            [G[4 - tx:12 - tx, 2 - ty:4 - ty].reshape(256, 128) for ty in range(3)], axis=1
        )
        part = lax.dot_general(window, feat3, TN, preferred_element_type=F32)
        for ty in range(3):
            rows = part[ty * 128:(ty + 1) * 128].reshape(nchip, 2, 8, 384)
            for tz in range(3):
                at = ((tx * 3 + ty) * 3 + tz) * 8
                for k in range(2):
                    T[k, :, at:at + 8, :] = rows[:, k, :, tz * 128:(tz + 1) * 128]
        part_rows = pl.ds(tx * 72, 80 if tx == 2 else 72)
        XS[:, part_rows, :] = T[1 - core, :, part_rows, :].astype(BF16)
        xcopies.append(remote(XS.at[:, part_rows, :], XR.at[:, part_rows, :], xs.at[tx], xr.at[tx], g, other))
        xcopies[-1].start()

    l_wf.wait()
    for h in far:
        h.wait_recv()

    @pl.when(g == 0)
    def _():
        G[0:2] = jnp.zeros((2,) + G.shape[1:], BF16)

    @pl.when(g == ngrp - 1)
    def _():
        G[12:14] = jnp.zeros((2,) + G.shape[1:], BF16)

    @pl.when(c == 0)
    def _():
        G[0:2, 0:1] = jnp.zeros((2, 1, 16, 128), BF16)
        G[12:14, 0:1] = jnp.zeros((2, 1, 16, 128), BF16)

    @pl.when(c == nchan - 1)
    def _():
        G[0:2, 3:4] = jnp.zeros((2, 1, 16, 128), BF16)
        G[12:14, 3:4] = jnp.zeros((2, 1, 16, 128), BF16)

    lhs = jnp.concatenate(
        [
            G[2 - tx:14 - tx, 2 - ty:4 - ty].reshape(384, 128)
            for tx in range(3)
            for ty in range(3)
        ],
        axis=1,
    )
    rhs = jnp.concatenate(
        [WF[tx, ty].reshape(384, 128) for tx in range(3) for ty in range(3)], axis=1
    )
    grown = lax.dot_general(lhs, rhs, NT, preferred_element_type=F32)
    z_at = lax.broadcasted_iota(jnp.int32, (384, 128), 0) % 16
    up = jnp.where(z_at < 15, pltpu.roll(grown[:, 0:128], 383, 0), 0.0)
    down = jnp.where(z_at > 0, pltpu.roll(grown[:, 256:384], 1, 0), 0.0)
    IG[...] = grown[:, 128:256] + up + down

    for x in xcopies:
        x.wait_recv()
    T[core] = T[core] + XR[...].astype(F32)
    SS[...] = T[core].astype(BF16)

    def scopy(s, part):
        d = lax.rem(chip + s, nchip)
        rows = pl.ds(0, 128) if part == 0 else pl.ds(128, 96)
        return remote(
            SS.at[d, rows], SR.at[chip, rows], ss.at[part, d], sr.at[part, chip], g, 2 * d + core
        )

    for part in range(2):

        def ssend(s, _):
            scopy(s, part).start()
            return 0

        lax.fori_loop(1, nchip, ssend, 0)

    l_up.wait()
    coarse = jnp.zeros((48, 512), F32)
    for a in range(2):
        for b in range(2):
            cells = jnp.concatenate(
                [
                    jnp.concatenate(
                        [IG[pl.ds(((2 * i + a) * 2 + b) * 16 + k, 8, stride=2), :] for i in range(6)],
                        axis=0,
                    )
                    for k in range(2)
                ],
                axis=1,
            ).astype(BF16)
            weight = jnp.concatenate([UP[a, b, 0], UP[a, b, 1]], axis=1)
            coarse = coarse + lax.dot_general(cells, weight, NT, preferred_element_type=F32)
    row_of = lax.broadcasted_iota(jnp.int32, (48, 512), 0)
    outside = ((row_of < 8) & (g == 0)) | ((row_of >= 40) & (g == ngrp - 1))
    coarse = jnp.where(outside, 0.0, coarse)
    low = lax.broadcasted_iota(jnp.int32, (8, 128), 1) < 64
    for q in range(4):
        block = coarse[:, q * 128:(q + 1) * 128]
        turned = pltpu.roll(block, 64, 1)
        for half in range(2):
            same, swap = (block, turned) if half == 0 else (turned, block)
            d = 2 * q + half
            for k in range(2):
                pair = []
                for i in (2 * k, 2 * k + 1):
                    s0, s1, s2 = (i + 2) * 8, (i + 1) * 8, i * 8
                    first = jnp.where(low, same[s0:s0 + 8], swap[s1:s1 + 8])
                    pair.append(jnp.concatenate([first, same[s2:s2 + 8]], axis=1))
                PS[2 * d + k] = jnp.concatenate(pair, axis=0).astype(BF16)

    def pcopy(s):
        d = group_of(s)
        return remote(PS.at[d], PR.at[c + 1], ps.at[d], pr.at[c], g, d)

    def psend(s, _):
        pcopy(s).start()
        return 0

    lax.fori_loop(1, nchan, psend, 0)
    PR[c + 1] = PS[c]

    for w in wcopies:
        w.wait_recv()

    def precv(s, _):
        o = group_of(s)
        remote(PS.at[o], PR.at[o + 1], ps.at[o], pr.at[o], g, o).wait_recv()
        return 0

    lax.fori_loop(1, nchan, precv, 0)
    rows = (nchan + 2) * 16
    slab = PR[...].reshape(rows, 256).astype(F32)
    k_of = lax.broadcasted_iota(jnp.int32, (rows, 256), 0) % 8
    SA[0] = jnp.where(k_of < 7, pltpu.roll(slab, rows - 1, 0), 0.0).astype(BF16).reshape(SA.shape[1:])
    SA[1] = PR[...]
    SA[2] = jnp.where(k_of > 0, pltpu.roll(slab, 1, 0), 0.0).astype(BF16).reshape(SA.shape[1:])
    lhs = jnp.concatenate(
        [
            SA[tz, 2 - ty:2 - ty + nchan].reshape(nchan * 16, 256)
            for ty in range(3)
            for tz in range(3)
        ],
        axis=1,
    )
    part = jnp.dot(lhs, WP[...].reshape(9 * 256, 512), preferred_element_type=F32)
    FS[...] = part.astype(BF16).reshape(FS.shape)

    def fcopy(s):
        d = group_of(s)
        return remote(FS.at[d], FR.at[c], fs.at[d], fr.at[c], g, d)

    def fsend(s, _):
        fcopy(s).start()
        return 0

    lax.fori_loop(1, nchan, fsend, 0)
    FR[c] = FS[c]

    for part in range(2):
        low_row, count = (0, 128) if part == 0 else (128, 96)
        total = T[core, chip, low_row:low_row + count, :]

        def srecv(s, acc):
            o = lax.rem(chip + s, nchip)
            rows = pl.ds(low_row, count)
            remote(
                SS.at[o, rows], SR.at[o, rows], ss.at[part, o], sr.at[part, o], g, 2 * o + core
            ).wait_recv()
            return acc + SR[o, low_row:low_row + count, :].astype(F32)

        total = lax.fori_loop(1, nchip, srecv, total)
        if count < 128:
            total = jnp.concatenate([total, jnp.zeros((128 - count, 128), F32)], axis=0)
        flipped = total.T
        VT[part] = flipped.reshape(VT.shape[1:])
        YS[part] = flipped.astype(BF16).reshape(YS.shape[1:])

        def ysend(s, _):
            ycopy(s, part).start()
            return 0

        lax.fori_loop(1, ny, ysend, 0)

    halves = []
    for part in range(2):

        def yrecv(s, acc):
            o = lax.rem(y + s, ny)
            remote(
                YS.at[part, o], YR.at[part, o], ys.at[part, o], yr.at[part, o], o * ZHI + zh, c
            ).wait_recv()
            return acc + YR[part, o].astype(F32)

        halves.append(lax.fori_loop(1, ny, yrecv, VT[part, y]))
    v2 = jnp.concatenate(halves, axis=1)
    for q in range(ZHI):
        ZS[q] = jnp.concatenate([v2[4 * q:4 * q + 4], jnp.zeros((4, 256), F32)], axis=0)

    def zcopy(s):
        d = lax.rem(zh + s, ZHI)
        return remote(ZS.at[d], ZR.at[zh], zs.at[d], zr.at[zh], y * ZHI + d, c)

    def zsend(s, _):
        zcopy(s).start()
        return 0

    lax.fori_loop(1, ZHI, zsend, 0)

    def frecv(s, _):
        o = group_of(s)
        remote(FS.at[o], FR.at[o], fs.at[o], fr.at[o], g, o).wait_recv()
        return 0

    lax.fori_loop(1, nchan, frecv, 0)
    for k in range(2):
        acc = FR[k].astype(F32)
        for p in range(1, nchan // 2):
            acc = acc + FR[2 * p + k].astype(F32)
        gh_out[k * 16:(k + 1) * 16, :] = acc.astype(BF16)

    for h in near + far:
        h.wait_send()
    for w in wcopies:
        w.wait_send()
    for x in xcopies:
        x.wait_send()

    def sent_group(s, _):
        pcopy(s).wait_send()
        fcopy(s).wait_send()
        return 0

    def sent_chip(s, _):
        scopy(s, 0).wait_send()
        scopy(s, 1).wait_send()
        return 0

    def sent_y(s, _):
        ycopy(s, 0).wait_send()
        ycopy(s, 1).wait_send()
        return 0

    def sent_z(s, _):
        zcopy(s).wait_send()
        return 0

    lax.fori_loop(1, nchan, sent_group, 0)
    lax.fori_loop(1, nchip, sent_chip, 0)
    lax.fori_loop(1, ny, sent_y, 0)
    lax.fori_loop(1, ZHI, sent_z, 0)

    def zrecv(s, acc):
        o = lax.rem(zh + s, ZHI)
        remote(ZS.at[o], ZR.at[o], zs.at[o], zr.at[o], y * ZHI + o, c).wait_recv()
        return acc + ZR[o]

    v3 = lax.fori_loop(1, ZHI, zrecv, ZS[zh])
    for t in range(27):
        tg_out[t] = v3[0:4, 8 * t:8 * t + 8]


def body(grad_out, feat_full, filters_full, upsample_weight, filters_half):
    nchan = lax.axis_size("chan")
    ny = lax.axis_size("grp") // ZHI
    nchip = nchan // 2
    wide = filters_half.shape[3]
    turned = jnp.swapaxes(filters_half, 3, 4)
    V = pltpu.VMEM
    D = pltpu.SemaphoreType.DMA
    anyspace = pl.BlockSpec(memory_space=pl.ANY)
    vmem = pl.BlockSpec(memory_space=pltpu.VMEM)
    grad_half, taps = pl.pallas_call(
        kernel,
        out_shape=(
            jax.ShapeDtypeStruct((32, wide), BF16),
            jax.ShapeDtypeStruct((27, 4, 8), F32),
        ),
        in_specs=[anyspace] * 5,
        out_specs=(vmem, vmem),
        scratch_shapes=[
            V((14, 4, 16, 128), BF16),
            V((8, 2, 16, 128), BF16),
            V((3, 3, 3, 128, 128), BF16),
            V((2, 2, 2, wide, 128), BF16),
            V((3, 3, 256, wide), BF16),
            V((384, 128), F32),
            V((2, nchip, 224, 128), F32),
            V((nchip, 224, 128), BF16),
            V((nchip, 224, 128), BF16),
            V((nchip, 224, 128), BF16),
            V((nchip, 224, 128), BF16),
            V((nchan, 16, 256), BF16),
            V((nchan + 2, 16, 256), BF16),
            V((3, nchan + 2, 16, 256), BF16),
            V((nchan, 16, wide), BF16),
            V((nchan, 16, wide), BF16),
            V((2, ny, 16, 128), F32),
            V((2, ny, 16, 128), BF16),
            V((2, ny, 16, 128), BF16),
            V((ZHI, 8, 256), F32),
            V((ZHI, 8, 256), F32),
            D((7,)),
            D((9,)), D((9,)),
            D((9,)), D((9,)),
            D((3,)), D((3,)),
            D((3,)), D((3,)),
            D((2, nchip)), D((2, nchip)),
            D((nchan,)), D((nchan,)),
            D((nchan,)), D((nchan,)),
            D((2, ny)), D((2, ny)),
            D((ZHI,)), D((ZHI,)),
        ],
        compiler_params=pltpu.CompilerParams(collective_id=0, has_side_effects=True),
    )(grad_out, feat_full, filters_full, upsample_weight, turned)
    return grad_half.reshape(1, 4, 8, wide), taps.reshape(3, 3, 3, 4, 8)


def solution(mesh):
    in_specs = (
        P("grp", "chan", None, None),
        P("grp", "chan", None, None),
        P(),
        P(),
        P(None, None, None, None, "chan"),
    )
    out_specs = (P("chan", "grp", None, None), P(None, None, None, "grp", "chan"))
    return jax.shard_map(body, mesh=mesh, in_specs=in_specs, out_specs=out_specs, check_vma=False)
```

```python
import jax
import jax.numpy as jnp
from jax import lax
from jax.experimental import pallas as pl
from jax.experimental.pallas import tpu as pltpu
from jax.sharding import PartitionSpec as P

TAP_ROW = {1: 0, 0: 80, 2: 152}
F32 = jnp.float32
BF16 = jnp.bfloat16
MESH = pl.DeviceIdType.MESH
NT = (((1,), (1,)), ((), ()))
TN = (((0,), (0,)), ((), ()))
ZHI = 4


def kernel(
    go, fe, wf, uw, wh,
    gh_out, tg_out,
    G, FE, WF, UP, WP, IG,
    T, XS, XR, SS, SR,
    PS, PR, SA, FS, FR,
    VT, YS, YR, ZS, ZR,
    lsem, hs, hr, hs2, hr2, ws, wr, xs, xr, ss, sr, ps, pr, fs, fr, ys, yr, zs, zr,
):
    g = lax.axis_index("grp")
    c = lax.axis_index("chan")
    ngrp = lax.axis_size("grp")
    nchan = lax.axis_size("chan")
    nchip = nchan // 2
    ny = ngrp // ZHI
    y, zh = g // ZHI, lax.rem(g, ZHI)
    chip, core = c // 2, lax.rem(c, 2)

    def dev(gi, ci):
        return {"grp": gi, "chan": ci}

    def remote(src, dst, send, recv, gi, ci):
        return pltpu.make_async_remote_copy(
            src_ref=src, dst_ref=dst, send_sem=send, recv_sem=recv,
            device_id=dev(gi, ci), device_id_type=MESH,
        )

    other = c + 1 - 2 * core

    def group_of(s):
        return lax.rem(c + s, nchan)

    def ygrp(s):
        return lax.rem(y + s, ny) * ZHI + zh

    def zgrp(s):
        return y * ZHI + lax.rem(zh + s, ZHI)

    def ycopy(s):
        d = lax.rem(y + s, ny)
        return remote(YS.at[d], YR.at[y], ys.at[d], yr.at[y], d * ZHI + zh, c)

    def scopy(s, part):
        d = lax.rem(chip + s, nchip)
        rows = pl.ds(0, 80) if part == 0 else pl.ds(80, 144)
        return remote(
            SS.at[d, rows], SR.at[chip, rows], ss.at[part, d], sr.at[part, chip], g, 2 * d + core
        )

    def tap_sums(tx):
        window = jnp.concatenate(
            [G[4 - tx:12 - tx, 2 - ty:4 - ty].reshape(256, 128) for ty in range(3)], axis=1
        )
        part = lax.dot_general(window, feat3, TN, preferred_element_type=F32)
        for ty in range(3):
            rows = part[ty * 128:(ty + 1) * 128].reshape(nchip, 2, 8, 384)
            for tz in range(3):
                at = TAP_ROW[tx] + (ty * 3 + tz) * 8
                for k in range(2):
                    T[k, :, at:at + 8, :] = rows[:, k, :, tz * 128:(tz + 1) * 128]

    def to_partner(part):
        rows = slice(0, 80) if part == 0 else slice(80, 224)
        XS[:, rows, :] = T[1 - core, :, rows, :].astype(BF16)
        copy = remote(XS.at[:, rows, :], XR.at[:, rows, :], xs.at[part], xr.at[part], g, other)
        copy.start()
        return copy

    def to_owners(copy, part):
        rows = slice(0, 80) if part == 0 else slice(80, 224)
        copy.wait_recv()
        summed = T[core, :, rows, :] + XR[:, rows, :].astype(F32)
        T[core, :, rows, :] = summed
        SS[:, rows, :] = summed.astype(BF16)

        def ssend(s, _):
            scopy(s, part).start()
            return 0

        lax.fori_loop(1, nchip, ssend, 0)

    l_go = pltpu.make_async_copy(go, G.at[3:11, 1:3], lsem.at[0])
    l_wh = [
        pltpu.make_async_copy(
            wh.at[t], WP.at[:, :, pl.ds(pl.multiple_of((2 - t) * 64 + core * 32, 32), 32), :], lsem.at[1 + t]
        )
        for t in range(3)
    ]
    l_fe = pltpu.make_async_copy(fe, FE, lsem.at[4])
    l_wf = pltpu.make_async_copy(wf, WF, lsem.at[5])
    l_up = pltpu.make_async_copy(uw, UP, lsem.at[6])
    l_go.start()
    l_fe.start()
    for t in range(3):
        l_wh[t].start()
    l_wf.start()
    l_up.start()

    barrier = pltpu.get_barrier_semaphore()

    def hello(gi, ci):
        pl.semaphore_signal(barrier, inc=1, device_id=dev(gi, ci), device_id_type=MESH)

    def hello_group(s, _):
        hello(g, group_of(s))
        return 0

    def hello_y(s, _):
        hello(ygrp(s), c)
        return 0

    def hello_z(s, _):
        hello(zgrp(s), c)
        return 0

    for dg in (1, ngrp - 1):
        for dc in (1, nchan - 1, 0):
            hello(lax.rem(g + dg, ngrp), group_of(dc))
    lax.fori_loop(1, ny, hello_y, 0)
    lax.fori_loop(1, ZHI, hello_z, 0)
    lax.fori_loop(1, nchan, hello_group, 0)

    PR[0] = jnp.zeros(PR.shape[1:], BF16)
    PR[nchan + 1] = jnp.zeros(PR.shape[1:], BF16)
    WP[:, :, 192:256, :] = jnp.zeros((3, 3, 64, WP.shape[3]), BF16)
    T[:, :, 72:80, :] = jnp.zeros((2, nchip, 8, 128), F32)
    l_fe.wait()
    feat = FE[...].reshape(256, 128).astype(F32)
    z_of = lax.broadcasted_iota(jnp.int32, (256, 128), 0) % 16
    before = jnp.where(z_of > 0, pltpu.roll(feat, 1, 0), 0.0)
    after = jnp.where(z_of < 15, pltpu.roll(feat, 255, 0), 0.0)
    feat3 = jnp.concatenate([before, feat, after], axis=1).astype(BF16)
    l_go.wait()

    pl.semaphore_wait(barrier, (nchan - 1) + (ny - 1) + (ZHI - 1) + 6)

    ysrc = {0: (1, 3), 1: (2, 3), 2: (1, 2)}
    ydst = {0: (1, 3), 1: (0, 1), 2: (3, 4)}
    gstep = {0: 0, 1: 1, 2: ngrp - 1}
    cstep = {0: 0, 1: 1, 2: nchan - 1}

    def halo(a, b, src, dst, send, recv):
        return remote(
            G.at[src[0]:src[1], ysrc[b][0]:ysrc[b][1]],
            G.at[dst[0]:dst[1], ydst[b][0]:ydst[b][1]],
            send.at[a * 3 + b], recv.at[a * 3 + b],
            lax.rem(g + gstep[a], ngrp), group_of(cstep[b]),
        )

    near_src = {0: (3, 11), 1: (10, 11), 2: (3, 4)}
    near_dst = {0: (3, 11), 1: (2, 3), 2: (11, 12)}
    far_src = {1: (8, 10), 2: (4, 6)}
    far_dst = {1: (0, 2), 2: (12, 14)}
    near = [
        halo(a, b, near_src[a], near_dst[a], hs, hr)
        for a, b in ((0, 1), (0, 2), (1, 1), (1, 2), (2, 1), (2, 2), (1, 0), (2, 0))
    ]
    far = [
        halo(a, b, far_src[a], far_dst[a], hs2, hr2)
        for a, b in ((1, 1), (1, 2), (2, 1), (2, 2), (1, 0), (2, 0))
    ]
    for h in near:
        h.start()
    for h in far:
        h.start()
    wcopies = []
    for t in range(3):
        l_wh[t].wait()
        rows = WP.at[:, :, pl.ds(pl.multiple_of((2 - t) * 64 + core * 32, 32), 32), :]
        wcopies.append(remote(rows, rows, ws.at[t], wr.at[t], g, other))
        wcopies[-1].start()
    near[0].wait_recv()
    near[1].wait_recv()

    @pl.when(c == 0)
    def _():
        G[3:11, 0:1] = jnp.zeros((8, 1, 16, 128), BF16)

    @pl.when(c == nchan - 1)
    def _():
        G[3:11, 3:4] = jnp.zeros((8, 1, 16, 128), BF16)

    tap_sums(1)
    xcopy0 = to_partner(0)
    to_owners(xcopy0, 0)

    for h in near[2:]:
        h.wait_recv()

    @pl.when(g == 0)
    def _():
        G[2:3] = jnp.zeros((1,) + G.shape[1:], BF16)

    @pl.when(g == ngrp - 1)
    def _():
        G[11:12] = jnp.zeros((1,) + G.shape[1:], BF16)

    @pl.when(c == 0)
    def _():
        G[2:3, 0:1] = jnp.zeros((1, 1, 16, 128), BF16)
        G[11:12, 0:1] = jnp.zeros((1, 1, 16, 128), BF16)

    @pl.when(c == nchan - 1)
    def _():
        G[2:3, 3:4] = jnp.zeros((1, 1, 16, 128), BF16)
        G[11:12, 3:4] = jnp.zeros((1, 1, 16, 128), BF16)

    tap_sums(0)
    tap_sums(2)
    xcopy1 = to_partner(1)

    l_wf.wait()
    for h in far:
        h.wait_recv()

    @pl.when(g == 0)
    def _():
        G[0:2] = jnp.zeros((2,) + G.shape[1:], BF16)

    @pl.when(g == ngrp - 1)
    def _():
        G[12:14] = jnp.zeros((2,) + G.shape[1:], BF16)

    @pl.when(c == 0)
    def _():
        G[0:2, 0:1] = jnp.zeros((2, 1, 16, 128), BF16)
        G[12:14, 0:1] = jnp.zeros((2, 1, 16, 128), BF16)

    @pl.when(c == nchan - 1)
    def _():
        G[0:2, 3:4] = jnp.zeros((2, 1, 16, 128), BF16)
        G[12:14, 3:4] = jnp.zeros((2, 1, 16, 128), BF16)

    lhs = jnp.concatenate(
        [
            G[2 - tx:14 - tx, 2 - ty:4 - ty].reshape(384, 128)
            for tx in range(3)
            for ty in range(3)
        ],
        axis=1,
    )
    rhs = jnp.concatenate(
        [WF[tx, ty].reshape(384, 128) for tx in range(3) for ty in range(3)], axis=1
    )
    grown = lax.dot_general(lhs, rhs, NT, preferred_element_type=F32)
    z_at = lax.broadcasted_iota(jnp.int32, (384, 128), 0) % 16
    up = jnp.where(z_at < 15, pltpu.roll(grown[:, 0:128], 383, 0), 0.0)
    down = jnp.where(z_at > 0, pltpu.roll(grown[:, 256:384], 1, 0), 0.0)
    IG[...] = grown[:, 128:256] + up + down

    l_up.wait()
    coarse = jnp.zeros((48, 512), F32)
    for a in range(2):
        for b in range(2):
            cells = jnp.concatenate(
                [
                    jnp.concatenate(
                        [IG[pl.ds(((2 * i + a) * 2 + b) * 16 + k, 8, stride=2), :] for i in range(6)],
                        axis=0,
                    )
                    for k in range(2)
                ],
                axis=1,
            ).astype(BF16)
            weight = jnp.concatenate([UP[a, b, 0], UP[a, b, 1]], axis=1)
            coarse = coarse + lax.dot_general(cells, weight, NT, preferred_element_type=F32)
    row_of = lax.broadcasted_iota(jnp.int32, (48, 512), 0)
    outside = ((row_of < 8) & (g == 0)) | ((row_of >= 40) & (g == ngrp - 1))
    coarse = jnp.where(outside, 0.0, coarse)
    low = lax.broadcasted_iota(jnp.int32, (8, 128), 1) < 64
    for q in range(4):
        block = coarse[:, q * 128:(q + 1) * 128]
        turned = pltpu.roll(block, 64, 1)
        for half in range(2):
            same, swap = (block, turned) if half == 0 else (turned, block)
            d = 2 * q + half
            for k in range(2):
                at = [coarse_row * 8 for coarse_row in range(2 * k, 2 * k + 4)]
                pair = [
                    jnp.where(low, same[at[r]:at[r] + 8], swap[at[r + 1]:at[r + 1] + 8]) for r in (0, 2)
                ]
                PS[2 * d + k] = jnp.concatenate(pair, axis=0).astype(BF16)

    def pcopy(s):
        d = group_of(s)
        return remote(PS.at[d], PR.at[c + 1], ps.at[d], pr.at[c], g, d)

    def psend(s, _):
        pcopy(s).start()
        return 0

    lax.fori_loop(1, nchan, psend, 0)
    PR[c + 1] = PS[c]
    to_owners(xcopy1, 1)

    for w in wcopies:
        w.wait_recv()

    def precv(s, _):
        o = group_of(s)
        remote(PS.at[o], PR.at[o + 1], ps.at[o], pr.at[o], g, o).wait_recv()
        return 0

    lax.fori_loop(1, nchan, precv, 0)
    rows = (nchan + 2) * 8
    slab = PR[...].astype(F32)
    slab = jnp.concatenate([slab[:, 0:8, :], slab[:, 8:16, :]], axis=2).reshape(rows, 256)
    k_of = lax.broadcasted_iota(jnp.int32, (rows, 256), 0) % 8
    shifted = (
        jnp.where(k_of < 7, pltpu.roll(slab, rows - 1, 0), 0.0),
        slab,
        jnp.where(k_of > 0, pltpu.roll(slab, 1, 0), 0.0),
    )
    for tz in range(3):
        pair = [v.reshape(nchan + 2, 8, 256) for v in (shifted[tz], pltpu.roll(shifted[tz], 192, 1))]
        SA[tz] = jnp.concatenate(pair, axis=1).astype(BF16)
    lhs = jnp.concatenate(
        [
            SA[tz, 2 - ty:2 - ty + nchan].reshape(nchan * 16, 256)
            for ty in range(3)
            for tz in range(3)
        ],
        axis=1,
    )
    part = jnp.dot(lhs, WP[...].reshape(9 * 256, 512), preferred_element_type=F32)
    FS[...] = part.astype(BF16).reshape(FS.shape)

    def fcopy(s):
        d = group_of(s)
        return remote(FS.at[d], FR.at[c], fs.at[d], fr.at[c], g, d)

    def fsend(s, _):
        fcopy(s).start()
        return 0

    lax.fori_loop(1, nchan, fsend, 0)
    FR[c] = FS[c]

    sums = []
    for part in range(2):
        low_row, count = (0, 80) if part == 0 else (80, 144)

        def srecv(s, acc):
            o = lax.rem(chip + s, nchip)
            rows = pl.ds(low_row, count)
            remote(
                SS.at[o, rows], SR.at[o, rows], ss.at[part, o], sr.at[part, o], g, 2 * o + core
            ).wait_recv()
            return acc + SR[o, low_row:low_row + count, :].astype(F32)

        sums.append(lax.fori_loop(1, nchip, srecv, T[core, chip, low_row:low_row + count, :]))
    flipped = jnp.concatenate(sums + [jnp.zeros((32, 128), F32)], axis=0).T
    VT[...] = flipped.reshape(VT.shape)
    YS[...] = flipped.astype(BF16).reshape(YS.shape)

    def ysend(s, _):
        ycopy(s).start()
        return 0

    lax.fori_loop(1, ny, ysend, 0)

    def yrecv(s, acc):
        o = lax.rem(y + s, ny)
        remote(YS.at[o], YR.at[o], ys.at[o], yr.at[o], o * ZHI + zh, c).wait_recv()
        return acc + YR[o].astype(F32)

    v2 = lax.fori_loop(1, ny, yrecv, VT[y])
    for q in range(ZHI):
        ZS[q] = jnp.concatenate([v2[4 * q:4 * q + 4], jnp.zeros((4, 256), F32)], axis=0)

    def zcopy(s):
        d = lax.rem(zh + s, ZHI)
        return remote(ZS.at[d], ZR.at[zh], zs.at[d], zr.at[zh], y * ZHI + d, c)

    def zsend(s, _):
        zcopy(s).start()
        return 0

    lax.fori_loop(1, ZHI, zsend, 0)

    def frecv(s, _):
        o = group_of(s)
        remote(FS.at[o], FR.at[o], fs.at[o], fr.at[o], g, o).wait_recv()
        return 0

    lax.fori_loop(1, nchan, frecv, 0)
    for k in range(2):
        acc = FR[k].astype(F32)
        for p in range(1, nchan // 2):
            acc = acc + FR[2 * p + k].astype(F32)
        gh_out[k * 16:(k + 1) * 16, :] = acc.astype(BF16)

    for h in near + far:
        h.wait_send()
    for w in wcopies:
        w.wait_send()
    xcopy0.wait_send()
    xcopy1.wait_send()

    def sent_group(s, _):
        pcopy(s).wait_send()
        fcopy(s).wait_send()
        return 0

    def sent_chip(s, _):
        scopy(s, 0).wait_send()
        scopy(s, 1).wait_send()
        return 0

    def sent_y(s, _):
        ycopy(s).wait_send()
        return 0

    def sent_z(s, _):
        zcopy(s).wait_send()
        return 0

    lax.fori_loop(1, nchan, sent_group, 0)
    lax.fori_loop(1, nchip, sent_chip, 0)
    lax.fori_loop(1, ny, sent_y, 0)
    lax.fori_loop(1, ZHI, sent_z, 0)

    def zrecv(s, acc):
        o = lax.rem(zh + s, ZHI)
        remote(ZS.at[o], ZR.at[o], zs.at[o], zr.at[o], y * ZHI + o, c).wait_recv()
        return acc + ZR[o]

    v3 = lax.fori_loop(1, ZHI, zrecv, ZS[zh])
    for tx in range(3):
        for t in range(9):
            at = TAP_ROW[tx] + 8 * t
            tg_out[tx * 9 + t] = v3[0:4, at:at + 8]


def body(grad_out, feat_full, filters_full, upsample_weight, filters_half):
    nchan = lax.axis_size("chan")
    ny = lax.axis_size("grp") // ZHI
    nchip = nchan // 2
    wide = filters_half.shape[3]
    turned = jnp.swapaxes(filters_half, 3, 4)
    V = pltpu.VMEM
    D = pltpu.SemaphoreType.DMA
    anyspace = pl.BlockSpec(memory_space=pl.ANY)
    vmem = pl.BlockSpec(memory_space=pltpu.VMEM)
    grad_half, taps = pl.pallas_call(
        kernel,
        out_shape=(
            pltpu.VMEM((32, wide), BF16),
            pltpu.VMEM((27, 4, 8), F32),
        ),
        in_specs=[anyspace] * 5,
        out_specs=(vmem, vmem),
        scratch_shapes=[
            V((14, 4, 16, 128), BF16),
            V((8, 2, 16, 128), BF16),
            V((3, 3, 3, 128, 128), BF16),
            V((2, 2, 2, wide, 128), BF16),
            V((3, 3, 256, wide), BF16),
            V((384, 128), F32),
            V((2, nchip, 224, 128), F32),
            V((nchip, 224, 128), BF16),
            V((nchip, 224, 128), BF16),
            V((nchip, 224, 128), BF16),
            V((nchip, 224, 128), BF16),
            V((nchan, 16, 128), BF16),
            V((nchan + 2, 16, 128), BF16),
            V((3, nchan + 2, 16, 256), BF16),
            V((nchan, 16, wide), BF16),
            V((nchan, 16, wide), BF16),
            V((ny, 16, 256), F32),
            V((ny, 16, 256), BF16),
            V((ny, 16, 256), BF16),
            V((ZHI, 8, 256), F32),
            V((ZHI, 8, 256), F32),
            D((7,)),
            D((9,)), D((9,)),
            D((9,)), D((9,)),
            D((3,)), D((3,)),
            D((2,)), D((2,)),
            D((2, nchip)), D((2, nchip)),
            D((nchan,)), D((nchan,)),
            D((nchan,)), D((nchan,)),
            D((ny,)), D((ny,)),
            D((ZHI,)), D((ZHI,)),
        ],
        compiler_params=pltpu.CompilerParams(collective_id=0, has_side_effects=True),
    )(grad_out, feat_full, filters_full, upsample_weight, turned)
    return grad_half.reshape(1, 4, 8, wide), taps.reshape(3, 3, 3, 4, 8)


def solution(mesh):
    in_specs = (
        P("grp", "chan", None, None),
        P("grp", "chan", None, None),
        P(),
        P(),
        P(None, None, None, None, "chan"),
    )
    out_specs = (P("chan", "grp", None, None), P(None, None, None, "grp", "chan"))
    return jax.shard_map(body, mesh=mesh, in_specs=in_specs, out_specs=out_specs, check_vma=False)
```

```python
import jax
import jax.numpy as jnp
from jax import lax
from jax.experimental import pallas as pl
from jax.experimental.pallas import tpu as pltpu
from jax.sharding import PartitionSpec as P

TAP_ROW = {1: 0, 0: 80, 2: 152}
F32 = jnp.float32
BF16 = jnp.bfloat16
MESH = pl.DeviceIdType.MESH
NT = (((1,), (1,)), ((), ()))
TN = (((0,), (0,)), ((), ()))
ZHI = 4


def kernel(
    go, fe, wf, uw, wh,
    gh_out, tg_out,
    G, FE, F3, WF, UP, WP, IG,
    T, XS, XR, SS, SR,
    PS, PR, SA, FS, FR,
    VT, YS, YR, ZS, ZR,
    lsem, es, er, ns, nr, qs, qr, rs, rr, ws, wr, xs, xr, ss, sr, ps, pr, fs, fr, ys, yr, zs, zr,
):
    g = lax.axis_index("grp")
    c = lax.axis_index("chan")
    ngrp = lax.axis_size("grp")
    nchan = lax.axis_size("chan")
    nchip = nchan // 2
    ny = ngrp // ZHI
    y, zh = g // ZHI, lax.rem(g, ZHI)
    chip, core = c // 2, lax.rem(c, 2)

    def dev(gi, ci):
        return {"grp": gi, "chan": ci}

    def remote(src, dst, send, recv, gi, ci):
        return pltpu.make_async_remote_copy(
            src_ref=src, dst_ref=dst, send_sem=send, recv_sem=recv,
            device_id=dev(gi, ci), device_id_type=MESH,
        )

    other = c + 1 - 2 * core

    def group_of(s):
        return lax.rem(c + s, nchan)

    def ygrp(s):
        return lax.rem(y + s, ny) * ZHI + zh

    def zgrp(s):
        return y * ZHI + lax.rem(zh + s, ZHI)

    def sent(ref, sem):
        remote(ref, ref, sem, sem, g, other).wait_send()

    def arrived(ref, sem):
        remote(ref, ref, sem, sem, g, other).wait_recv()

    def ycopy(s):
        d = lax.rem(y + s, ny)
        return remote(YS.at[d], YR.at[y], ys, yr, d * ZHI + zh, c)

    def tap_rows(part):
        return slice(0, 80) if part == 0 else slice(80, 224)

    def tap_sums(txs, feat3):
        planes = []
        for tx in txs:
            if tx == 0:
                last = jnp.where(g == ngrp - 1, jnp.zeros((1, 2, 16, 128), BF16), G[11:12, 1:3])
                window = jnp.concatenate([G[4:11, 1:3], last], axis=0)
            elif tx == 1:
                window = G[3:11, 1:3]
            else:
                first = jnp.where(g == 0, jnp.zeros((1, 2, 16, 128), BF16), G[2:3, 1:3])
                window = jnp.concatenate([first, G[3:10, 1:3]], axis=0)
            planes.append(window.reshape(256, 128))
        part = lax.dot_general(
            jnp.concatenate(planes, axis=1), feat3, TN, preferred_element_type=F32
        )
        for n, tx in enumerate(txs):
            rows = part[n * 128:(n + 1) * 128].reshape(nchip, 2, 8, 9 * 128)
            for t in range(9):
                at = TAP_ROW[tx] + t * 8
                for k in range(2):
                    T[k, :, at:at + 8, :] = rows[:, k, :, t * 128:(t + 1) * 128]

    def to_partner(part):
        rows = tap_rows(part)
        XS[:, rows, :] = T[1 - core, :, rows, :].astype(BF16)
        remote(XS.at[:, rows, :], XR.at[:, rows, :], xs.at[part], xr.at[part], g, other).start()

    def to_owners(part):
        rows = tap_rows(part)
        arrived(XR.at[:, rows, :], xr.at[part])
        summed = T[core, :, rows, :] + XR[:, rows, :].astype(F32)
        T[core, :, rows, :] = summed
        SS[:, rows, :] = summed.astype(BF16)

        def ssend(s, _):
            d = lax.rem(chip + s, nchip)
            remote(
                SS.at[d, rows], SR.at[chip, rows], ss.at[part], sr.at[part], g, 2 * d + core
            ).start()
            return 0

        lax.fori_loop(1, nchip, ssend, 0)

    def along_z(cells):
        z_of = lax.broadcasted_iota(jnp.int32, cells.shape, 0) % 16
        before = jnp.where(z_of > 0, pltpu.roll(cells, 1, 0), 0.0)
        after = jnp.where(z_of < 15, pltpu.roll(cells, cells.shape[0] - 1, 0), 0.0)
        return jnp.concatenate([before, cells, after], axis=1).astype(BF16)

    l_go = pltpu.make_async_copy(go, G.at[3:11, 1:3], lsem.at[0])
    l_fe = pltpu.make_async_copy(fe, FE.at[:, 1:3], lsem.at[1])
    own_rows = [WP.at[:, :, pl.ds(pl.multiple_of((2 - t) * 64 + core * 32, 32), 32), :] for t in range(3)]
    l_wh = [pltpu.make_async_copy(wh.at[t], own_rows[t], lsem.at[2 + t]) for t in range(3)]
    l_wf = pltpu.make_async_copy(wf, WF, lsem.at[5])
    l_up = pltpu.make_async_copy(uw, UP, lsem.at[6])
    l_fe.start()
    l_go.start()
    for t in range(3):
        l_wh[t].start()
    l_wf.start()
    l_up.start()

    barrier = pltpu.get_barrier_semaphore()

    def hello(gi, ci):
        pl.semaphore_signal(barrier, inc=1, device_id=dev(gi, ci), device_id_type=MESH)

    def hello_group(s, _):
        hello(g, group_of(s))
        return 0

    def hello_y(s, _):
        hello(ygrp(s), c)
        return 0

    def hello_z(s, _):
        hello(zgrp(s), c)
        return 0

    for dg in (1, ngrp - 1):
        hello(lax.rem(g + dg, ngrp), c)
    lax.fori_loop(1, ny, hello_y, 0)
    lax.fori_loop(1, ZHI, hello_z, 0)
    lax.fori_loop(1, nchan, hello_group, 0)

    PR[0] = jnp.zeros(PR.shape[1:], BF16)
    PR[nchan + 1] = jnp.zeros(PR.shape[1:], BF16)
    WP[:, :, 192:256, :] = jnp.zeros((3, 3, 64, WP.shape[3]), BF16)
    T[:, :, 72:80, :] = jnp.zeros((2, nchip, 8, 128), F32)
    l_fe.wait()
    F3[:, 1:3] = along_z(FE[:, 1:3].reshape(256, 128).astype(F32)).reshape(8, 2, 16, 384)
    l_go.wait()

    pl.semaphore_wait(barrier, (nchan - 1) + (ny - 1) + (ZHI - 1) + 2)

    upper, lower = lax.rem(g + 1, ngrp), lax.rem(g + ngrp - 1, ngrp)
    right, left = group_of(1), group_of(nchan - 1)
    remote(FE.at[:, 2:3], FE.at[:, 0:1], es, er, g, right).start()
    remote(FE.at[:, 1:2], FE.at[:, 3:4], es, er, g, left).start()
    remote(G.at[10:11, 1:3], G.at[2:3, 1:3], ns, nr, upper, c).start()
    remote(G.at[3:4, 1:3], G.at[11:12, 1:3], ns, nr, lower, c).start()
    remote(G.at[8:10, 1:3], G.at[0:2, 1:3], qs, qr, upper, c).start()
    remote(G.at[4:6, 1:3], G.at[12:14, 1:3], qs, qr, lower, c).start()
    remote(G.at[3:11, 2:3], G.at[3:11, 0:1], rs, rr, g, right).start()
    remote(G.at[3:11, 1:2], G.at[3:11, 3:4], rs, rr, g, left).start()
    arrived(FE.at[:, 1:3], er)
    for row, edge in ((0, 0), (3, nchan - 1)):
        shifted = along_z(FE[:, row:row + 1].reshape(128, 128).astype(F32)).reshape(8, 1, 16, 384)
        F3[:, row:row + 1] = jnp.where(c == edge, jnp.zeros_like(shifted), shifted)

    feat3 = jnp.concatenate([F3[:, ty:ty + 2].reshape(256, 384) for ty in range(3)], axis=1)
    tap_sums((1,), feat3)
    to_partner(0)
    arrived(G.at[0:1, 0:4], nr)
    tap_sums((0, 2), feat3)
    to_partner(1)
    arrived(G.at[0:2, 0:4], qr)
    for planes in ((0, 3), (11, 14)):
        at = slice(planes[0], planes[1])
        remote(G.at[at, 2:3], G.at[at, 0:1], rs, rr, g, right).start()
        remote(G.at[at, 1:2], G.at[at, 3:4], rs, rr, g, left).start()
    to_owners(0)
    for t in range(3):
        l_wh[t].wait()
        remote(own_rows[t], own_rows[t], ws, wr, g, other).start()
    to_owners(1)
    l_wf.wait()
    l_up.wait()
    sent(G.at[0:7, 0:4], rs)
    arrived(G.at[0:7, 0:4], rr)

    @pl.when(g == 0)
    def _():
        G[0:3] = jnp.zeros((3,) + G.shape[1:], BF16)

    @pl.when(g == ngrp - 1)
    def _():
        G[11:14] = jnp.zeros((3,) + G.shape[1:], BF16)

    @pl.when(c == 0)
    def _():
        G[:, 0:1] = jnp.zeros((14, 1, 16, 128), BF16)

    @pl.when(c == nchan - 1)
    def _():
        G[:, 3:4] = jnp.zeros((14, 1, 16, 128), BF16)

    lhs = jnp.concatenate(
        [
            G[2 - tx:14 - tx, 2 - ty:4 - ty].reshape(384, 128)
            for tx in range(3)
            for ty in range(3)
        ],
        axis=1,
    )
    rhs = jnp.concatenate(
        [WF[tx, ty].reshape(384, 128) for tx in range(3) for ty in range(3)], axis=1
    )
    grown = lax.dot_general(lhs, rhs, NT, preferred_element_type=F32)
    z_at = lax.broadcasted_iota(jnp.int32, (384, 128), 0) % 16
    up = jnp.where(z_at < 15, pltpu.roll(grown[:, 0:128], 383, 0), 0.0)
    down = jnp.where(z_at > 0, pltpu.roll(grown[:, 256:384], 1, 0), 0.0)
    IG[...] = grown[:, 128:256] + up + down

    coarse = jnp.zeros((48, 512), F32)
    for a in range(2):
        for b in range(2):
            cells = jnp.concatenate(
                [
                    jnp.concatenate(
                        [IG[pl.ds(((2 * i + a) * 2 + b) * 16 + k, 8, stride=2), :] for i in range(6)],
                        axis=0,
                    )
                    for k in range(2)
                ],
                axis=1,
            ).astype(BF16)
            weight = jnp.concatenate([UP[a, b, 0], UP[a, b, 1]], axis=1)
            coarse = coarse + lax.dot_general(cells, weight, NT, preferred_element_type=F32)
    row_of = lax.broadcasted_iota(jnp.int32, (48, 512), 0)
    outside = ((row_of < 8) & (g == 0)) | ((row_of >= 40) & (g == ngrp - 1))
    coarse = jnp.where(outside, 0.0, coarse)
    low = lax.broadcasted_iota(jnp.int32, (8, 128), 1) < 64
    for q in range(4):
        block = coarse[:, q * 128:(q + 1) * 128]
        turned = pltpu.roll(block, 64, 1)
        for half in range(2):
            same, swap = (block, turned) if half == 0 else (turned, block)
            d = 2 * q + half
            for k in range(2):
                at = [coarse_row * 8 for coarse_row in range(2 * k, 2 * k + 4)]
                pair = [
                    jnp.where(low, same[at[r]:at[r] + 8], swap[at[r + 1]:at[r + 1] + 8]) for r in (0, 2)
                ]
                PS[2 * d + k] = jnp.concatenate(pair, axis=0).astype(BF16)

    def psend(s, _):
        d = group_of(s)
        remote(PS.at[d], PR.at[c + 1], ps, pr, g, d).start()
        return 0

    lax.fori_loop(1, nchan, psend, 0)
    PR[c + 1] = PS[c]
    for part in range(2):
        arrived(SR.at[0:7, tap_rows(part)], sr.at[part])
    total = T[core, chip]
    for s in range(1, nchan // 2):
        total = total + SR[lax.rem(chip + s, nchip)].astype(F32)
    flipped = jnp.concatenate([total, jnp.zeros((32, 128), F32)], axis=0).T
    VT[...] = flipped.reshape(VT.shape)
    YS[...] = flipped.astype(BF16).reshape(YS.shape)

    def ysend(s, _):
        ycopy(s).start()
        return 0

    lax.fori_loop(1, ny, ysend, 0)

    arrived(WP.at[:, :, 0:96, :], wr)
    arrived(PR.at[0:15], pr)
    rows = (nchan + 2) * 8
    slab = PR[...].astype(F32)
    slab = jnp.concatenate([slab[:, 0:8, :], slab[:, 8:16, :]], axis=2).reshape(rows, 256)
    k_of = lax.broadcasted_iota(jnp.int32, (rows, 256), 0) % 8
    shifted = (
        jnp.where(k_of < 7, pltpu.roll(slab, rows - 1, 0), 0.0),
        slab,
        jnp.where(k_of > 0, pltpu.roll(slab, 1, 0), 0.0),
    )
    for tz in range(3):
        pair = [v.reshape(nchan + 2, 8, 256) for v in (shifted[tz], pltpu.roll(shifted[tz], 192, 1))]
        SA[tz] = jnp.concatenate(pair, axis=1).astype(BF16)
    lhs = jnp.concatenate(
        [
            SA[tz, 2 - ty:2 - ty + nchan].reshape(nchan * 16, 256)
            for ty in range(3)
            for tz in range(3)
        ],
        axis=1,
    )
    part = jnp.dot(lhs, WP[...].reshape(9 * 256, 512), preferred_element_type=F32)
    FS[...] = part.astype(BF16).reshape(FS.shape)

    def fsend(s, _):
        d = group_of(s)
        remote(FS.at[d], FR.at[c], fs, fr, g, d).start()
        return 0

    lax.fori_loop(1, nchan, fsend, 0)
    FR[c] = FS[c]

    arrived(YR.at[0:7], yr)
    v2 = VT[y]
    for s in range(1, YR.shape[0]):
        v2 = v2 + YR[lax.rem(y + s, ny)].astype(F32)
    for q in range(ZHI):
        ZS[q] = jnp.concatenate([v2[4 * q:4 * q + 4], jnp.zeros((4, 256), F32)], axis=0)

    def zsend(s, _):
        d = lax.rem(zh + s, ZHI)
        remote(ZS.at[d], ZR.at[zh], zs, zr, y * ZHI + d, c).start()
        return 0

    lax.fori_loop(1, ZHI, zsend, 0)

    arrived(FR.at[0:15], fr)
    for k in range(2):
        acc = FR[k].astype(F32)
        for p in range(1, nchan // 2):
            acc = acc + FR[2 * p + k].astype(F32)
        gh_out[k * 16:(k + 1) * 16, :] = acc.astype(BF16)

    sent(FE.at[:, 1:3], es)
    sent(G.at[0:1, 0:4], ns)
    sent(G.at[0:2, 0:4], qs)
    sent(WP.at[:, :, 0:96, :], ws)
    for part in range(2):
        sent(XS.at[:, tap_rows(part), :], xs.at[part])
        sent(SS.at[0:7, tap_rows(part)], ss.at[part])
    sent(PS.at[0:15], ps)
    sent(FS.at[0:15], fs)
    sent(YS.at[0:7], ys)
    sent(ZS.at[0:3], zs)

    arrived(ZR.at[0:3], zr)
    v3 = ZS[zh]
    for s in range(1, ZHI):
        v3 = v3 + ZR[lax.rem(zh + s, ZHI)]
    for tx in range(3):
        for t in range(9):
            at = TAP_ROW[tx] + 8 * t
            tg_out[tx * 9 + t] = v3[0:4, at:at + 8]


def body(grad_out, feat_full, filters_full, upsample_weight, filters_half):
    nchan = lax.axis_size("chan")
    ny = lax.axis_size("grp") // ZHI
    nchip = nchan // 2
    wide = filters_half.shape[3]
    turned = jnp.swapaxes(filters_half, 3, 4)
    V = pltpu.VMEM
    D = pltpu.SemaphoreType.DMA
    anyspace = pl.BlockSpec(memory_space=pl.ANY)
    vmem = pl.BlockSpec(memory_space=pltpu.VMEM)
    grad_half, taps = pl.pallas_call(
        kernel,
        out_shape=(
            pltpu.VMEM((32, wide), BF16),
            pltpu.VMEM((27, 4, 8), F32),
        ),
        in_specs=[anyspace] * 5,
        out_specs=(vmem, vmem),
        scratch_shapes=[
            V((14, 4, 16, 128), BF16),
            V((8, 4, 16, 128), BF16),
            V((8, 4, 16, 384), BF16),
            V((3, 3, 3, 128, 128), BF16),
            V((2, 2, 2, wide, 128), BF16),
            V((3, 3, 256, wide), BF16),
            V((384, 128), F32),
            V((2, nchip, 224, 128), F32),
            V((nchip, 224, 128), BF16),
            V((nchip, 224, 128), BF16),
            V((nchip, 224, 128), BF16),
            V((nchip, 224, 128), BF16),
            V((nchan, 16, 128), BF16),
            V((nchan + 2, 16, 128), BF16),
            V((3, nchan + 2, 16, 256), BF16),
            V((nchan, 16, wide), BF16),
            V((nchan, 16, wide), BF16),
            V((ny, 16, 256), F32),
            V((ny, 16, 256), BF16),
            V((ny, 16, 256), BF16),
            V((ZHI, 8, 256), F32),
            V((ZHI, 8, 256), F32),
            D((7,)),
            D, D, D, D, D, D, D, D, D, D,
            D((2,)), D((2,)), D((2,)), D((2,)),
            D, D, D, D, D, D, D, D,
        ],
        compiler_params=pltpu.CompilerParams(collective_id=0, has_side_effects=True),
    )(grad_out, feat_full, filters_full, upsample_weight, turned)
    return grad_half.reshape(1, 4, 8, wide), taps.reshape(3, 3, 3, 4, 8)


def solution(mesh):
    in_specs = (
        P("grp", "chan", None, None),
        P("grp", "chan", None, None),
        P(),
        P(),
        P(None, None, None, None, "chan"),
    )
    out_specs = (P("chan", "grp", None, None), P(None, None, None, "grp", "chan"))
    return jax.shard_map(body, mesh=mesh, in_specs=in_specs, out_specs=out_specs, check_vma=False)
```

```python
import jax
import jax.numpy as jnp
from jax import lax
from jax.experimental import pallas as pl
from jax.experimental.pallas import tpu as pltpu
from jax.sharding import PartitionSpec as P

F32 = jnp.float32
BF16 = jnp.bfloat16
MESH = pl.DeviceIdType.MESH
NT = (((1,), (1,)), ((), ()))
TN = (((0,), (0,)), ((), ()))
ZHI = 4


def kernel(
    go, fe, wf, uw, wh,
    gh_out, tg_out,
    G, FE, F3, WF, UP, WP, IG,
    T, SS, SR,
    PS, PR, SA, FS, FR,
    VT, YS, YR, ZS, ZR,
    lsem, es, er, ns, nr, qs, qr, rs, rr, ws, wr, ss, sr, ps, pr, fs, fr, ys, yr, zs, zr,
):
    g = lax.axis_index("grp")
    c = lax.axis_index("chan")
    ngrp = lax.axis_size("grp")
    nchan = lax.axis_size("chan")
    nchip = nchan // 2
    ny = ngrp // ZHI
    y, zh = g // ZHI, lax.rem(g, ZHI)
    chip, core = c // 2, lax.rem(c, 2)

    def dev(gi, ci):
        return {"grp": gi, "chan": ci}

    def remote(src, dst, send, recv, gi, ci):
        return pltpu.make_async_remote_copy(
            src_ref=src, dst_ref=dst, send_sem=send, recv_sem=recv,
            device_id=dev(gi, ci), device_id_type=MESH,
        )

    other = c + 1 - 2 * core

    def group_of(s):
        return lax.rem(c + s, nchan)

    def ygrp(s):
        return lax.rem(y + s, ny) * ZHI + zh

    def zgrp(s):
        return y * ZHI + lax.rem(zh + s, ZHI)

    def sent(ref, sem):
        remote(ref, ref, sem, sem, g, other).wait_send()

    def arrived(ref, sem):
        remote(ref, ref, sem, sem, g, other).wait_recv()

    def ycopy(s):
        d = lax.rem(y + s, ny)
        return remote(YS.at[d], YR.at[y], ys, yr, d * ZHI + zh, c)

    def tap_rows(part):
        return slice(0, 40) if part == 0 else slice(40, 112)

    def tap_sums(tx, feat3):
        if tx == 0:
            last = jnp.where(g == ngrp - 1, jnp.zeros((1, 4, 16, 128), BF16), G[11:12, 1:5])
            window = jnp.concatenate([G[4:11, 1:5], last], axis=0)
        elif tx == 1:
            window = G[3:11, 1:5]
        else:
            first = jnp.where(g == 0, jnp.zeros((1, 4, 16, 128), BF16), G[2:3, 1:5])
            window = jnp.concatenate([first, G[3:10, 1:5]], axis=0)
        part = lax.dot_general(window.reshape(512, 128), feat3, TN, preferred_element_type=F32)
        rows = part.reshape(nchan, 8, 5 * 128)
        for n in range(5):
            if tx == 1:
                at = n * 8
            elif tx == 0:
                at = 40 if n == 0 else pl.multiple_of((5 + n - core) * 8, 8)
            else:
                at = pl.multiple_of((10 + n - core) * 8, 8)
            T[:, pl.ds(at, 8), :] = rows[:, :, n * 128:(n + 1) * 128]

    def to_owners(part):
        rows = tap_rows(part)
        SS[:, rows, :] = T[:, rows, :].astype(BF16)

        def ssend(s, _):
            d = group_of(s)
            remote(SS.at[d, rows], SR.at[c, rows], ss.at[part], sr.at[part], g, d).start()
            return 0

        lax.fori_loop(1, nchan, ssend, 0)

    def along_z(cells):
        z_of = lax.broadcasted_iota(jnp.int32, cells.shape, 0) % 16
        before = jnp.where(z_of > 0, pltpu.roll(cells, 1, 0), 0.0)
        after = jnp.where(z_of < 15, pltpu.roll(cells, cells.shape[0] - 1, 0), 0.0)
        return before.astype(BF16), cells.astype(BF16), after.astype(BF16)

    mine, theirs = pl.ds(1 + 2 * core, 2), pl.ds(3 - 2 * core, 2)
    inner_row, edge_row = pl.ds(2 + core, 1), pl.ds(1 + 3 * core, 1)
    far_row = pl.ds(5 - 5 * core, 1)
    facing, beyond = group_of(nchan + 2 * core - 1), group_of(nchan + 4 * core - 2)
    l_go = pltpu.make_async_copy(go, G.at[3:11, mine], lsem.at[0])
    l_fe = pltpu.make_async_copy(fe, FE.at[:, mine], lsem.at[1])
    own_rows = [WP.at[:, :, pl.ds(pl.multiple_of((2 - t) * 64 + core * 32, 32), 32), :] for t in range(3)]
    l_wh = [pltpu.make_async_copy(wh.at[t], own_rows[t], lsem.at[2 + t]) for t in range(3)]
    l_wf = pltpu.make_async_copy(wf, WF, lsem.at[5])
    l_up = pltpu.make_async_copy(uw, UP, lsem.at[6])
    l_fe.start()
    l_go.start()
    for t in range(3):
        l_wh[t].start()
    l_wf.start()
    l_up.start()

    barrier = pltpu.get_barrier_semaphore()

    def hello(gi, ci):
        pl.semaphore_signal(barrier, inc=1, device_id=dev(gi, ci), device_id_type=MESH)

    def hello_group(s, _):
        hello(g, group_of(s))
        return 0

    def hello_y(s, _):
        hello(ygrp(s), c)
        return 0

    def hello_z(s, _):
        hello(zgrp(s), c)
        return 0

    for dg in (1, ngrp - 1):
        hello(lax.rem(g + dg, ngrp), c)
        hello(lax.rem(g + dg, ngrp), other)
    lax.fori_loop(1, ny, hello_y, 0)
    lax.fori_loop(1, ZHI, hello_z, 0)
    lax.fori_loop(1, nchan, hello_group, 0)

    PR[0] = jnp.zeros(PR.shape[1:], BF16)
    PR[nchan + 1] = jnp.zeros(PR.shape[1:], BF16)
    WP[:, :, 192:256, :] = jnp.zeros((3, 3, 64, WP.shape[3]), BF16)
    def feature_rows(rows, count, edge):
        cells = count * 128
        for tz, shifted in enumerate(along_z(FE[:, rows].reshape(cells, 128).astype(F32))):
            shifted = shifted.reshape(8, count, 16, 128)
            if edge is not None:
                shifted = jnp.where(chip == edge, jnp.zeros_like(shifted), shifted)
            F3[tz, :, rows] = shifted

    l_fe.wait()
    feature_rows(mine, 2, None)
    l_go.wait()

    pl.semaphore_wait(barrier, (nchan - 1) + (ny - 1) + (ZHI - 1) + 4)

    upper, lower = lax.rem(g + 1, ngrp), lax.rem(g + ngrp - 1, ngrp)
    remote(FE.at[:, edge_row], FE.at[:, far_row], es, er, g, beyond).start()
    remote(FE.at[:, edge_row], FE.at[:, far_row], es, er, g, facing).start()
    remote(FE.at[:, mine], FE.at[:, mine], es, er, g, other).start()
    remote(G.at[3:11, mine], G.at[3:11, mine], es, er, g, other).start()
    for to in (other, c):
        remote(G.at[10:11, mine], G.at[2:3, mine], ns, nr, upper, to).start()
        remote(G.at[3:4, mine], G.at[11:12, mine], ns, nr, lower, to).start()
    remote(G.at[8:10, mine], G.at[0:2, mine], qs, qr, upper, c).start()
    remote(G.at[4:6, mine], G.at[12:14, mine], qs, qr, lower, c).start()
    remote(G.at[3:11, edge_row], G.at[3:11, far_row], rs, rr, g, facing).start()
    arrived(FE, er)
    feature_rows(theirs, 2, None)
    feature_rows(pl.ds(0, 1), 1, 0)
    feature_rows(pl.ds(5, 1), 1, nchip - 1)
    tiles = []
    for n in range(5):
        m = 4 * core + n
        tiles.append(F3[lax.rem(m, 3), :, pl.ds(m // 3, 4)].reshape(512, 128))
    feat3 = jnp.concatenate(tiles, axis=1)
    tap_sums(1, feat3)
    to_owners(0)
    arrived(G.at[0:2, 0:4], nr)
    tap_sums(0, feat3)
    tap_sums(2, feat3)
    to_owners(1)
    arrived(G.at[0:2, 0:4], qr)
    remote(G.at[0:3, edge_row], G.at[0:3, far_row], rs, rr, g, facing).start()
    remote(G.at[11:14, edge_row], G.at[11:14, far_row], rs, rr, g, facing).start()
    remote(G.at[0:2, inner_row], G.at[0:2, inner_row], rs, rr, g, other).start()
    remote(G.at[12:14, inner_row], G.at[12:14, inner_row], rs, rr, g, other).start()
    for t in range(3):
        l_wh[t].wait()
        remote(own_rows[t], own_rows[t], ws, wr, g, other).start()
    l_wf.wait()
    l_up.wait()
    sent(G.at[0:3], rs)
    arrived(G.at[0:3], rr)

    @pl.when(g == 0)
    def _():
        G[0:3] = jnp.zeros((3,) + G.shape[1:], BF16)

    @pl.when(g == ngrp - 1)
    def _():
        G[11:14] = jnp.zeros((3,) + G.shape[1:], BF16)

    @pl.when(chip == 0)
    def _():
        G[:, 0:1] = jnp.zeros((14, 1, 16, 128), BF16)

    @pl.when(chip == nchip - 1)
    def _():
        G[:, 5:6] = jnp.zeros((14, 1, 16, 128), BF16)

    lhs = jnp.concatenate(
        [
            G[2 - tx:14 - tx, pl.ds(2 + 2 * core - ty, 2)].reshape(384, 128)
            for tx in range(3)
            for ty in range(3)
        ],
        axis=1,
    )
    rhs = jnp.concatenate(
        [WF[tx, ty].reshape(384, 128) for tx in range(3) for ty in range(3)], axis=1
    )
    grown = lax.dot_general(lhs, rhs, NT, preferred_element_type=F32)
    z_at = lax.broadcasted_iota(jnp.int32, (384, 128), 0) % 16
    up = jnp.where(z_at < 15, pltpu.roll(grown[:, 0:128], 383, 0), 0.0)
    down = jnp.where(z_at > 0, pltpu.roll(grown[:, 256:384], 1, 0), 0.0)
    IG[...] = grown[:, 128:256] + up + down

    coarse = jnp.zeros((48, 512), F32)
    for a in range(2):
        for b in range(2):
            cells = jnp.concatenate(
                [
                    jnp.concatenate(
                        [IG[pl.ds(((2 * i + a) * 2 + b) * 16 + k, 8, stride=2), :] for i in range(6)],
                        axis=0,
                    )
                    for k in range(2)
                ],
                axis=1,
            ).astype(BF16)
            weight = jnp.concatenate([UP[a, b, 0], UP[a, b, 1]], axis=1)
            coarse = coarse + lax.dot_general(cells, weight, NT, preferred_element_type=F32)
    row_of = lax.broadcasted_iota(jnp.int32, (48, 512), 0)
    outside = ((row_of < 8) & (g == 0)) | ((row_of >= 40) & (g == ngrp - 1))
    coarse = jnp.where(outside, 0.0, coarse)
    low = lax.broadcasted_iota(jnp.int32, (8, 128), 1) < 64
    for q in range(4):
        block = coarse[:, q * 128:(q + 1) * 128]
        turned = pltpu.roll(block, 64, 1)
        for half in range(2):
            same, swap = (block, turned) if half == 0 else (turned, block)
            d = 2 * q + half
            for k in range(2):
                at = [coarse_row * 8 for coarse_row in range(2 * k, 2 * k + 4)]
                pair = [
                    jnp.where(low, same[at[r]:at[r] + 8], swap[at[r + 1]:at[r + 1] + 8]) for r in (0, 2)
                ]
                PS[2 * d + k] = jnp.concatenate(pair, axis=0).astype(BF16)

    def psend(s, _):
        d = group_of(s)
        remote(PS.at[d], PR.at[c + 1], ps, pr, g, d).start()
        return 0

    lax.fori_loop(1, nchan, psend, 0)
    PR[c + 1] = PS[c]
    for part in range(2):
        arrived(SR.at[0:15, tap_rows(part)], sr.at[part])
    SR[c] = SS[c]
    sums = []
    for k in range(2):
        total = SR[k].astype(F32)
        for p in range(1, nchan // 2):
            total = total + SR[2 * p + k].astype(F32)
        sums.append(total)
    flipped = jnp.concatenate(sums + [jnp.zeros((32, 128), F32)], axis=0).T
    VT[...] = flipped.reshape(VT.shape)
    YS[...] = flipped.astype(BF16).reshape(YS.shape)

    def ysend(s, _):
        ycopy(s).start()
        return 0

    lax.fori_loop(1, ny, ysend, 0)

    arrived(WP.at[:, :, 0:96, :], wr)
    arrived(PR.at[0:15], pr)
    rows = (nchan + 2) * 8
    slab = PR[...].astype(F32)
    slab = jnp.concatenate([slab[:, 0:8, :], slab[:, 8:16, :]], axis=2).reshape(rows, 256)
    k_of = lax.broadcasted_iota(jnp.int32, (rows, 256), 0) % 8
    shifted = (
        jnp.where(k_of < 7, pltpu.roll(slab, rows - 1, 0), 0.0),
        slab,
        jnp.where(k_of > 0, pltpu.roll(slab, 1, 0), 0.0),
    )
    for tz in range(3):
        pair = [v.reshape(nchan + 2, 8, 256) for v in (shifted[tz], pltpu.roll(shifted[tz], 192, 1))]
        SA[tz] = jnp.concatenate(pair, axis=1).astype(BF16)
    lhs = jnp.concatenate(
        [
            SA[tz, 2 - ty:2 - ty + nchan].reshape(nchan * 16, 256)
            for ty in range(3)
            for tz in range(3)
        ],
        axis=1,
    )
    part = jnp.dot(lhs, WP[...].reshape(9 * 256, 512), preferred_element_type=F32)
    FS[...] = part.astype(BF16).reshape(FS.shape)

    def fsend(s, _):
        d = group_of(s)
        remote(FS.at[d], FR.at[c], fs, fr, g, d).start()
        return 0

    lax.fori_loop(1, nchan, fsend, 0)
    FR[c] = FS[c]

    arrived(YR.at[0:7], yr)
    v2 = VT[y]
    for s in range(1, YR.shape[0]):
        v2 = v2 + YR[lax.rem(y + s, ny)].astype(F32)
    for q in range(ZHI):
        ZS[q] = jnp.concatenate([v2[4 * q:4 * q + 4], jnp.zeros((4, 256), F32)], axis=0)

    def zsend(s, _):
        d = lax.rem(zh + s, ZHI)
        remote(ZS.at[d], ZR.at[zh], zs, zr, y * ZHI + d, c).start()
        return 0

    lax.fori_loop(1, ZHI, zsend, 0)

    arrived(FR.at[0:15], fr)
    for k in range(2):
        acc = FR[k].astype(F32)
        for p in range(1, nchan // 2):
            acc = acc + FR[2 * p + k].astype(F32)
        gh_out[k * 16:(k + 1) * 16, :] = acc.astype(BF16)

    sent(FE, es)
    sent(G.at[0:2, 0:4], ns)
    sent(G.at[0:2, 0:4], qs)
    sent(WP.at[:, :, 0:96, :], ws)
    for part in range(2):
        sent(SS.at[0:15, tap_rows(part)], ss.at[part])
    sent(PS.at[0:15], ps)
    sent(FS.at[0:15], fs)
    sent(YS.at[0:7], ys)
    sent(ZS.at[0:3], zs)

    arrived(ZR.at[0:3], zr)
    v3 = ZS[zh]
    for s in range(1, ZHI):
        v3 = v3 + ZR[lax.rem(zh + s, ZHI)]
    for m in range(9):
        base = (
            m * 8 + (40 if m < 5 else 112),
            m * 8 if m < 5 else 112 + (m - 4) * 8,
            (10 + m) * 8 if m < 4 else 112 + (5 + m) * 8,
        )
        for tx in range(3):
            tg_out[tx * 9 + m] = v3[0:4, base[tx]:base[tx] + 8]


def body(grad_out, feat_full, filters_full, upsample_weight, filters_half):
    nchan = lax.axis_size("chan")
    ny = lax.axis_size("grp") // ZHI
    wide = filters_half.shape[3]
    turned = jnp.swapaxes(filters_half, 3, 4)
    V = pltpu.VMEM
    D = pltpu.SemaphoreType.DMA
    anyspace = pl.BlockSpec(memory_space=pl.ANY)
    vmem = pl.BlockSpec(memory_space=pltpu.VMEM)
    grad_half, taps = pl.pallas_call(
        kernel,
        out_shape=(
            pltpu.VMEM((32, wide), BF16),
            pltpu.VMEM((27, 4, 8), F32),
        ),
        in_specs=[anyspace] * 5,
        out_specs=(vmem, vmem),
        scratch_shapes=[
            V((14, 6, 16, 128), BF16),
            V((8, 6, 16, 128), BF16),
            V((3, 8, 6, 16, 128), BF16),
            V((3, 3, 3, 128, 128), BF16),
            V((2, 2, 2, wide, 128), BF16),
            V((3, 3, 256, wide), BF16),
            V((384, 128), F32),
            V((nchan, 120, 128), F32),
            V((nchan, 112, 128), BF16),
            V((nchan, 112, 128), BF16),
            V((nchan, 16, 128), BF16),
            V((nchan + 2, 16, 128), BF16),
            V((3, nchan + 2, 16, 256), BF16),
            V((nchan, 16, wide), BF16),
            V((nchan, 16, wide), BF16),
            V((ny, 16, 256), F32),
            V((ny, 16, 256), BF16),
            V((ny, 16, 256), BF16),
            V((ZHI, 8, 256), F32),
            V((ZHI, 8, 256), F32),
            D((7,)),
            D, D, D, D, D, D, D, D, D, D,
            D((2,)), D((2,)),
            D, D, D, D, D, D, D, D,
        ],
        compiler_params=pltpu.CompilerParams(collective_id=0, has_side_effects=True),
    )(grad_out, feat_full, filters_full, upsample_weight, turned)
    return grad_half.reshape(1, 4, 8, wide), taps.reshape(3, 3, 3, 4, 8)


def solution(mesh):
    in_specs = (
        P("grp", "chan", None, None),
        P("grp", "chan", None, None),
        P(),
        P(),
        P(None, None, None, None, "chan"),
    )
    out_specs = (P("chan", "grp", None, None), P(None, None, None, "grp", "chan"))
    return jax.shard_map(body, mesh=mesh, in_specs=in_specs, out_specs=out_specs, check_vma=False)
```

```python
import jax
import jax.numpy as jnp
from jax import lax
from jax.experimental import pallas as pl
from jax.experimental.pallas import tpu as pltpu
from jax.sharding import PartitionSpec as P

TAP_ROW = {
    (tx, ty): {1: {1: 0, 0: 32, 2: 56}, 0: {0: 80, 1: 104, 2: 128}, 2: {0: 152, 1: 176, 2: 200}}[tx][ty]
    for tx in range(3)
    for ty in range(3)
}
TAP_PART = (slice(0, 32), slice(32, 80), slice(80, 224))
FAR_CHIPS = ((1, 2), (0, 2), (1, 1), (1, 3), (0, 1), (0, 3), (1, 0))
FAR_Y = (4, 3, 5, 2, 6, 1, 7)
FAR_Z = (2, 1, 3)
F32 = jnp.float32
BF16 = jnp.bfloat16
MESH = pl.DeviceIdType.MESH
NT = (((1,), (1,)), ((), ()))
TN = (((0,), (0,)), ((), ()))
ZHI = 4


def kernel(
    go, fe, wf, uw, wh,
    gh_out, tg_out,
    G, FE, F3, WF, UP, WP, IG,
    T, XS, XR, SS, SR,
    PS, PR, SA, FS, FR,
    VT, YS, YR, ZS, ZR,
    lsem, es, er, ns, nr, qs, qr, rs, rr, ws, wr, xs, xr, ss, sr, ps, pr, fs, fr, ys, yr, zs, zr,
):
    g = lax.axis_index("grp")
    c = lax.axis_index("chan")
    ngrp = lax.axis_size("grp")
    nchan = lax.axis_size("chan")
    nchip = nchan // 2
    ny = ngrp // ZHI
    y, zh = g // ZHI, lax.rem(g, ZHI)
    chip, core = c // 2, lax.rem(c, 2)

    def dev(gi, ci):
        return {"grp": gi, "chan": ci}

    def remote(src, dst, send, recv, gi, ci):
        return pltpu.make_async_remote_copy(
            src_ref=src, dst_ref=dst, send_sem=send, recv_sem=recv,
            device_id=dev(gi, ci), device_id_type=MESH,
        )

    other = c + 1 - 2 * core

    def group_of(s):
        return lax.rem(c + s, nchan)

    def ygrp(s):
        return lax.rem(y + s, ny) * ZHI + zh

    def zgrp(s):
        return y * ZHI + lax.rem(zh + s, ZHI)

    def sent(ref, sem):
        remote(ref, ref, sem, sem, g, other).wait_send()

    def arrived(ref, sem):
        remote(ref, ref, sem, sem, g, other).wait_recv()

    def ycopy(s):
        d = lax.rem(y + s, ny)
        return remote(YS.at[d], YR.at[y], ys, yr, d * ZHI + zh, c)

    def chip_at(dz, dx):
        return (chip // 4 + dz) % 2 * 4 + (chip % 4 + dx) % 4

    far_chips = [chip_at(dz, dx) for dz, dx in FAR_CHIPS]
    far_members = [2 * p + k for p in far_chips for k in range(2)] + [other]

    def tap_sums(txs, tys, feat3):
        planes = []
        for tx in txs:
            if tx == 0:
                last = jnp.where(g == ngrp - 1, jnp.zeros((1, 2, 16, 128), BF16), G[11:12, 1:3])
                window = jnp.concatenate([G[4:11, 1:3], last], axis=0)
            elif tx == 1:
                window = G[3:11, 1:3]
            else:
                first = jnp.where(g == 0, jnp.zeros((1, 2, 16, 128), BF16), G[2:3, 1:3])
                window = jnp.concatenate([first, G[3:10, 1:3]], axis=0)
            planes.append(window.reshape(256, 128))
        part = lax.dot_general(
            jnp.concatenate(planes, axis=1), feat3, TN, preferred_element_type=F32
        )
        for n, tx in enumerate(txs):
            rows = part[n * 128:(n + 1) * 128].reshape(nchip, 2, 8, feat3.shape[1])
            for m, ty in enumerate(tys):
                for tz in range(3):
                    at = TAP_ROW[tx, ty] + tz * 8
                    t = (m * 3 + tz) * 128
                    for k in range(2):
                        T[k, :, at:at + 8, :] = rows[:, k, :, t:t + 128]

    def to_partner(part):
        rows = TAP_PART[part]
        XS[:, rows, :] = T[1 - core, :, rows, :].astype(BF16)
        remote(XS.at[:, rows, :], XR.at[:, rows, :], xs.at[part], xr.at[part], g, other).start()

    def to_owners(part):
        rows = TAP_PART[part]
        arrived(XR.at[:, rows, :], xr.at[part])
        summed = T[core, :, rows, :] + XR[:, rows, :].astype(F32)
        T[core, :, rows, :] = summed
        SS[:, rows, :] = summed.astype(BF16)
        for d in far_chips:
            remote(
                SS.at[d, rows], SR.at[chip, rows], ss.at[part], sr.at[part], g, 2 * d + core
            ).start()

    def feat_rows(tys):
        return jnp.concatenate([F3[:, ty:ty + 2].reshape(256, 384) for ty in tys], axis=1)

    def along_z(cells):
        z_of = lax.broadcasted_iota(jnp.int32, cells.shape, 0) % 16
        before = jnp.where(z_of > 0, pltpu.roll(cells, 1, 0), 0.0)
        after = jnp.where(z_of < 15, pltpu.roll(cells, cells.shape[0] - 1, 0), 0.0)
        return jnp.concatenate([before, cells, after], axis=1).astype(BF16)

    l_go = pltpu.make_async_copy(go, G.at[3:11, 1:3], lsem.at[0])
    l_fe = pltpu.make_async_copy(fe, FE.at[:, 1:3], lsem.at[1])
    own_rows = [WP.at[:, :, pl.ds(pl.multiple_of((2 - t) * 64 + core * 32, 32), 32), :] for t in range(3)]
    l_wh = [pltpu.make_async_copy(wh.at[t], own_rows[t], lsem.at[2 + t]) for t in range(3)]
    l_wf = pltpu.make_async_copy(wf, WF, lsem.at[5])
    l_up = pltpu.make_async_copy(uw, UP, lsem.at[6])
    l_fe.start()
    l_go.start()
    for t in range(3):
        l_wh[t].start()
    l_wf.start()
    l_up.start()

    barrier = pltpu.get_barrier_semaphore()

    def hello(gi, ci):
        pl.semaphore_signal(barrier, inc=1, device_id=dev(gi, ci), device_id_type=MESH)

    def hello_group(s, _):
        hello(g, group_of(s))
        return 0

    def hello_y(s, _):
        hello(ygrp(s), c)
        return 0

    def hello_z(s, _):
        hello(zgrp(s), c)
        return 0

    for dg in (1, ngrp - 1):
        hello(lax.rem(g + dg, ngrp), c)
    lax.fori_loop(1, ny, hello_y, 0)
    lax.fori_loop(1, ZHI, hello_z, 0)
    lax.fori_loop(1, nchan, hello_group, 0)

    PR[0] = jnp.zeros(PR.shape[1:], BF16)
    PR[nchan + 1] = jnp.zeros(PR.shape[1:], BF16)
    WP[:, :, 192:256, :] = jnp.zeros((3, 3, 64, WP.shape[3]), BF16)
    T[:, :, 24:32, :] = jnp.zeros((2, nchip, 8, 128), F32)
    l_fe.wait()
    F3[:, 1:3] = along_z(FE[:, 1:3].reshape(256, 128).astype(F32)).reshape(8, 2, 16, 384)
    l_go.wait()
    tap_sums((1,), (1,), feat_rows((1,)))

    pl.semaphore_wait(barrier, (nchan - 1) + (ny - 1) + (ZHI - 1) + 2)

    upper, lower = lax.rem(g + 1, ngrp), lax.rem(g + ngrp - 1, ngrp)
    right, left = group_of(1), group_of(nchan - 1)
    remote(FE.at[:, 2:3], FE.at[:, 0:1], es, er, g, right).start()
    remote(FE.at[:, 1:2], FE.at[:, 3:4], es, er, g, left).start()
    remote(G.at[10:11, 1:3], G.at[2:3, 1:3], ns, nr, upper, c).start()
    remote(G.at[3:4, 1:3], G.at[11:12, 1:3], ns, nr, lower, c).start()
    remote(G.at[8:10, 1:3], G.at[0:2, 1:3], qs, qr, upper, c).start()
    remote(G.at[4:6, 1:3], G.at[12:14, 1:3], qs, qr, lower, c).start()
    remote(G.at[3:11, 2:3], G.at[3:11, 0:1], rs, rr, g, right).start()
    remote(G.at[3:11, 1:2], G.at[3:11, 3:4], rs, rr, g, left).start()
    to_partner(0)
    to_owners(0)
    arrived(FE.at[:, 1:3], er)
    for row, edge in ((0, 0), (3, nchan - 1)):
        shifted = along_z(FE[:, row:row + 1].reshape(128, 128).astype(F32)).reshape(8, 1, 16, 384)
        F3[:, row:row + 1] = jnp.where(c == edge, jnp.zeros_like(shifted), shifted)

    tap_sums((1,), (0, 2), feat_rows((0, 2)))
    to_partner(1)
    arrived(G.at[0:1, 0:4], nr)
    tap_sums((0, 2), (0, 1, 2), feat_rows((0, 1, 2)))
    to_partner(2)
    arrived(G.at[0:2, 0:4], qr)
    for planes in ((0, 3), (11, 14)):
        at = slice(planes[0], planes[1])
        remote(G.at[at, 2:3], G.at[at, 0:1], rs, rr, g, right).start()
        remote(G.at[at, 1:2], G.at[at, 3:4], rs, rr, g, left).start()
    to_owners(1)
    for t in range(3):
        l_wh[t].wait()
        remote(own_rows[t], own_rows[t], ws, wr, g, other).start()
    to_owners(2)
    l_wf.wait()
    l_up.wait()
    sent(G.at[0:7, 0:4], rs)
    arrived(G.at[0:7, 0:4], rr)

    @pl.when(g == 0)
    def _():
        G[0:3] = jnp.zeros((3,) + G.shape[1:], BF16)

    @pl.when(g == ngrp - 1)
    def _():
        G[11:14] = jnp.zeros((3,) + G.shape[1:], BF16)

    @pl.when(c == 0)
    def _():
        G[:, 0:1] = jnp.zeros((14, 1, 16, 128), BF16)

    @pl.when(c == nchan - 1)
    def _():
        G[:, 3:4] = jnp.zeros((14, 1, 16, 128), BF16)

    lhs = jnp.concatenate(
        [
            G[2 - tx:14 - tx, 2 - ty:4 - ty].reshape(384, 128)
            for tx in range(3)
            for ty in range(3)
        ],
        axis=1,
    )
    rhs = jnp.concatenate(
        [WF[tx, ty].reshape(384, 128) for tx in range(3) for ty in range(3)], axis=1
    )
    grown = lax.dot_general(lhs, rhs, NT, preferred_element_type=F32)
    z_at = lax.broadcasted_iota(jnp.int32, (384, 128), 0) % 16
    up = jnp.where(z_at < 15, pltpu.roll(grown[:, 0:128], 383, 0), 0.0)
    down = jnp.where(z_at > 0, pltpu.roll(grown[:, 256:384], 1, 0), 0.0)
    IG[...] = grown[:, 128:256] + up + down

    coarse = jnp.zeros((48, 512), F32)
    for a in range(2):
        for b in range(2):
            cells = jnp.concatenate(
                [
                    jnp.concatenate(
                        [IG[pl.ds(((2 * i + a) * 2 + b) * 16 + k, 8, stride=2), :] for i in range(6)],
                        axis=0,
                    )
                    for k in range(2)
                ],
                axis=1,
            ).astype(BF16)
            weight = jnp.concatenate([UP[a, b, 0], UP[a, b, 1]], axis=1)
            coarse = coarse + lax.dot_general(cells, weight, NT, preferred_element_type=F32)
    row_of = lax.broadcasted_iota(jnp.int32, (48, 512), 0)
    outside = ((row_of < 8) & (g == 0)) | ((row_of >= 40) & (g == ngrp - 1))
    coarse = jnp.where(outside, 0.0, coarse)
    low = lax.broadcasted_iota(jnp.int32, (8, 128), 1) < 64
    for q in range(4):
        block = coarse[:, q * 128:(q + 1) * 128]
        turned = pltpu.roll(block, 64, 1)
        for half in range(2):
            same, swap = (block, turned) if half == 0 else (turned, block)
            d = 2 * q + half
            for k in range(2):
                at = [coarse_row * 8 for coarse_row in range(2 * k, 2 * k + 4)]
                pair = [
                    jnp.where(low, same[at[r]:at[r] + 8], swap[at[r + 1]:at[r + 1] + 8]) for r in (0, 2)
                ]
                PS[2 * d + k] = jnp.concatenate(pair, axis=0).astype(BF16)

    for d in far_members:
        remote(PS.at[d], PR.at[c + 1], ps, pr, g, d).start()
    PR[c + 1] = PS[c]
    for part in range(3):
        arrived(SR.at[0:7, TAP_PART[part]], sr.at[part])
    total = T[core, chip]
    for s in range(1, nchan // 2):
        total = total + SR[lax.rem(chip + s, nchip)].astype(F32)
    flipped = jnp.concatenate([total, jnp.zeros((32, 128), F32)], axis=0).T
    VT[...] = flipped.reshape(VT.shape)
    YS[...] = flipped.astype(BF16).reshape(YS.shape)

    for s in FAR_Y:
        ycopy(s).start()

    arrived(WP.at[:, :, 0:96, :], wr)
    arrived(PR.at[0:15], pr)
    rows = (nchan + 2) * 8
    slab = PR[...].astype(F32)
    slab = jnp.concatenate([slab[:, 0:8, :], slab[:, 8:16, :]], axis=2).reshape(rows, 256)
    k_of = lax.broadcasted_iota(jnp.int32, (rows, 256), 0) % 8
    shifted = (
        jnp.where(k_of < 7, pltpu.roll(slab, rows - 1, 0), 0.0),
        slab,
        jnp.where(k_of > 0, pltpu.roll(slab, 1, 0), 0.0),
    )
    for tz in range(3):
        pair = [v.reshape(nchan + 2, 8, 256) for v in (shifted[tz], pltpu.roll(shifted[tz], 192, 1))]
        SA[tz] = jnp.concatenate(pair, axis=1).astype(BF16)
    lhs = jnp.concatenate(
        [
            SA[tz, 2 - ty:2 - ty + nchan].reshape(nchan * 16, 256)
            for ty in range(3)
            for tz in range(3)
        ],
        axis=1,
    )
    part = jnp.dot(lhs, WP[...].reshape(9 * 256, 512), preferred_element_type=F32)
    FS[...] = part.astype(BF16).reshape(FS.shape)

    for d in far_members:
        remote(FS.at[d], FR.at[c], fs, fr, g, d).start()
    FR[c] = FS[c]

    arrived(YR.at[0:7], yr)
    v2 = VT[y]
    for s in range(1, YR.shape[0]):
        v2 = v2 + YR[lax.rem(y + s, ny)].astype(F32)
    for q in range(ZHI):
        rows = v2[4 * q:4 * q + 4]
        ZS[q] = jnp.concatenate([rows[:, 0:128], rows[:, 128:256]], axis=0)
    for s in FAR_Z:
        d = lax.rem(zh + s, ZHI)
        remote(ZS.at[d], ZR.at[zh], zs, zr, y * ZHI + d, c).start()

    arrived(FR.at[0:15], fr)
    for k in range(2):
        acc = FR[k].astype(F32)
        for p in range(1, nchan // 2):
            acc = acc + FR[2 * p + k].astype(F32)
        gh_out[k * 16:(k + 1) * 16, :] = acc.astype(BF16)

    sent(FE.at[:, 1:3], es)
    sent(G.at[0:1, 0:4], ns)
    sent(G.at[0:2, 0:4], qs)
    sent(WP.at[:, :, 0:96, :], ws)
    for part in range(3):
        sent(XS.at[:, TAP_PART[part], :], xs.at[part])
        sent(SS.at[0:7, TAP_PART[part]], ss.at[part])
    sent(PS.at[0:15], ps)
    sent(FS.at[0:15], fs)
    sent(YS.at[0:7], ys)
    sent(ZS.at[0:3], zs)

    arrived(ZR.at[0:3], zr)
    v3 = ZS[zh]
    for s in range(1, ZHI):
        v3 = v3 + ZR[lax.rem(zh + s, ZHI)]
    for tx in range(3):
        for ty in range(3):
            for tz in range(3):
                at = TAP_ROW[tx, ty] + tz * 8
                row, lane = at // 128 * 4, at % 128
                tg_out[(tx * 3 + ty) * 3 + tz] = v3[row:row + 4, lane:lane + 8]


def body(grad_out, feat_full, filters_full, upsample_weight, filters_half):
    nchan = lax.axis_size("chan")
    ny = lax.axis_size("grp") // ZHI
    nchip = nchan // 2
    wide = filters_half.shape[3]
    turned = jnp.swapaxes(filters_half, 3, 4)
    V = pltpu.VMEM
    D = pltpu.SemaphoreType.DMA
    anyspace = pl.BlockSpec(memory_space=pl.ANY)
    vmem = pl.BlockSpec(memory_space=pltpu.VMEM)
    grad_half, taps = pl.pallas_call(
        kernel,
        out_shape=(
            pltpu.VMEM((32, wide), BF16),
            pltpu.VMEM((27, 4, 8), F32),
        ),
        in_specs=[anyspace] * 5,
        out_specs=(vmem, vmem),
        scratch_shapes=[
            V((14, 4, 16, 128), BF16),
            V((8, 4, 16, 128), BF16),
            V((8, 4, 16, 384), BF16),
            V((3, 3, 3, 128, 128), BF16),
            V((2, 2, 2, wide, 128), BF16),
            V((3, 3, 256, wide), BF16),
            V((384, 128), F32),
            V((2, nchip, 224, 128), F32),
            V((nchip, 224, 128), BF16),
            V((nchip, 224, 128), BF16),
            V((nchip, 224, 128), BF16),
            V((nchip, 224, 128), BF16),
            V((nchan, 16, 128), BF16),
            V((nchan + 2, 16, 128), BF16),
            V((3, nchan + 2, 16, 256), BF16),
            V((nchan, 16, wide), BF16),
            V((nchan, 16, wide), BF16),
            V((ny, 16, 256), F32),
            V((ny, 16, 256), BF16),
            V((ny, 16, 256), BF16),
            V((ZHI, 8, 128), F32),
            V((ZHI, 8, 128), F32),
            D((7,)),
            D, D, D, D, D, D, D, D, D, D,
            D((3,)), D((3,)), D((3,)), D((3,)),
            D, D, D, D, D, D, D, D,
        ],
        compiler_params=pltpu.CompilerParams(collective_id=0, has_side_effects=True),
    )(grad_out, feat_full, filters_full, upsample_weight, turned)
    return grad_half.reshape(1, 4, 8, wide), taps.reshape(3, 3, 3, 4, 8)


def solution(mesh):
    in_specs = (
        P("grp", "chan", None, None),
        P("grp", "chan", None, None),
        P(),
        P(),
        P(None, None, None, None, "chan"),
    )
    out_specs = (P("chan", "grp", None, None), P(None, None, None, "grp", "chan"))
    return jax.shard_map(body, mesh=mesh, in_specs=in_specs, out_specs=out_specs, check_vma=False)
```

```python
import jax
import jax.numpy as jnp
from jax import lax
from jax.experimental import pallas as pl
from jax.experimental.pallas import tpu as pltpu
from jax.sharding import PartitionSpec as P

ZHI = 4
TAP_ROW = {
    (tx, ty): {1: {1: 0, 0: 32, 2: 56}, 0: {0: 80, 1: 104, 2: 128}, 2: {0: 152, 1: 176, 2: 200}}[tx][ty]
    for tx in range(3)
    for ty in range(3)
}
TAP_PART = (slice(0, 32), slice(32, 80), slice(80, 224))
FAR_CHIPS = ((1, 2), (0, 2), (1, 1), (1, 3), (0, 1), (0, 3), (1, 0))
FAR_GROUPS = sorted(
    ((dy, dz) for dy in range(8) for dz in range(ZHI) if dy + dz > 0),
    key=lambda d: -(min(d[0], 8 - d[0]) + 2 * min(d[1], ZHI - d[1])),
)
F32 = jnp.float32
BF16 = jnp.bfloat16
MESH = pl.DeviceIdType.MESH
NT = (((1,), (1,)), ((), ()))
TN = (((0,), (0,)), ((), ()))


def kernel(
    go, fe, wf, uw, wh,
    gh_out, tg_out,
    G, FE, F3, WF, UP, WP, IG,
    T, XS, XR, SS, SR,
    PS, PR, SA, FS, FR,
    YS, YR,
    lsem, es, er, ns, nr, qs, qr, rs, rr, ws, wr, xs, xr, ss, sr, ps, pr, fs, fr, ys, yr, ready,
):
    g = lax.axis_index("grp")
    c = lax.axis_index("chan")
    ngrp = lax.axis_size("grp")
    nchan = lax.axis_size("chan")
    nchip = nchan // 2
    ny = ngrp // ZHI
    y, zh = g // ZHI, lax.rem(g, ZHI)
    chip, core = c // 2, lax.rem(c, 2)

    def dev(gi, ci):
        return {"grp": gi, "chan": ci}

    def remote(src, dst, send, recv, gi, ci):
        return pltpu.make_async_remote_copy(
            src_ref=src, dst_ref=dst, send_sem=send, recv_sem=recv,
            device_id=dev(gi, ci), device_id_type=MESH,
        )

    other = c + 1 - 2 * core

    def group_of(s):
        return lax.rem(c + s, nchan)

    def ygrp(s):
        return lax.rem(y + s, ny) * ZHI + zh

    def zgrp(s):
        return y * ZHI + lax.rem(zh + s, ZHI)

    def sent(ref, sem):
        remote(ref, ref, sem, sem, g, other).wait_send()

    def arrived(ref, sem):
        remote(ref, ref, sem, sem, g, other).wait_recv()

    def chip_at(dz, dx):
        return (chip // 4 + dz) % 2 * 4 + (chip % 4 + dx) % 4

    far_chips = [chip_at(dz, dx) for dz, dx in FAR_CHIPS]
    far_members = [2 * p + k for p in far_chips for k in range(2)] + [other]

    def tap_sums(txs, tys, feat3):
        planes = []
        for tx in txs:
            if tx == 0:
                last = jnp.where(g == ngrp - 1, jnp.zeros((1, 2, 16, 128), BF16), G[11:12, 1:3])
                window = jnp.concatenate([G[4:11, 1:3], last], axis=0)
            elif tx == 1:
                window = G[3:11, 1:3]
            else:
                first = jnp.where(g == 0, jnp.zeros((1, 2, 16, 128), BF16), G[2:3, 1:3])
                window = jnp.concatenate([first, G[3:10, 1:3]], axis=0)
            planes.append(window.reshape(256, 128))
        part = lax.dot_general(
            jnp.concatenate(planes, axis=1), feat3, TN, preferred_element_type=F32
        )
        for n, tx in enumerate(txs):
            rows = part[n * 128:(n + 1) * 128].reshape(nchip, 2, 8, feat3.shape[1])
            for m, ty in enumerate(tys):
                for tz in range(3):
                    at = TAP_ROW[tx, ty] + tz * 8
                    t = (m * 3 + tz) * 128
                    for k in range(2):
                        T[k, :, at:at + 8, :] = rows[:, k, :, t:t + 128]

    def to_partner(part):
        rows = TAP_PART[part]
        XS[:, rows, :] = T[1 - core, :, rows, :].astype(BF16)
        remote(XS.at[:, rows, :], XR.at[:, rows, :], xs.at[part], xr.at[part], g, other).start()

    def to_owners(part):
        rows = TAP_PART[part]
        arrived(XR.at[:, rows, :], xr.at[part])
        summed = T[core, :, rows, :] + XR[:, rows, :].astype(F32)
        T[core, :, rows, :] = summed
        SS[:, rows, :] = summed.astype(BF16)
        for d in far_chips:
            remote(
                SS.at[d, rows], SR.at[chip, rows], ss.at[part], sr.at[part], g, 2 * d + core
            ).start()

    def feat_rows(tys):
        return jnp.concatenate([F3[:, ty:ty + 2].reshape(256, 384) for ty in tys], axis=1)

    def along_z(cells):
        z_of = lax.broadcasted_iota(jnp.int32, cells.shape, 0) % 16
        before = jnp.where(z_of > 0, pltpu.roll(cells, 1, 0), 0.0)
        after = jnp.where(z_of < 15, pltpu.roll(cells, cells.shape[0] - 1, 0), 0.0)
        return jnp.concatenate([before, cells, after], axis=1).astype(BF16)

    l_go = pltpu.make_async_copy(go, G.at[3:11, 1:3], lsem.at[0])
    l_fe = pltpu.make_async_copy(fe, FE.at[:, 1:3], lsem.at[1])
    own_rows = [WP.at[:, :, pl.ds(pl.multiple_of((2 - t) * 64 + core * 32, 32), 32), :] for t in range(3)]
    l_wh = [pltpu.make_async_copy(wh.at[t], own_rows[t], lsem.at[2 + t]) for t in range(3)]
    l_wf = pltpu.make_async_copy(wf, WF, lsem.at[5])
    l_up = pltpu.make_async_copy(uw, UP, lsem.at[6])
    l_fe.start()
    l_go.start()
    for t in range(3):
        l_wh[t].start()
    l_wf.start()
    l_up.start()

    barrier = pltpu.get_barrier_semaphore()

    def hello(gi, ci):
        pl.semaphore_signal(barrier, inc=1, device_id=dev(gi, ci), device_id_type=MESH)

    def hello_group(s, _):
        hello(g, group_of(s))
        return 0

    def hello_y(s, _):
        hello(ygrp(s), c)
        return 0

    def hello_z(s, _):
        hello(zgrp(s), c)
        return 0

    for dg in (1, ngrp - 1):
        hello(lax.rem(g + dg, ngrp), c)
    lax.fori_loop(1, ny, hello_y, 0)
    lax.fori_loop(1, ZHI, hello_z, 0)
    lax.fori_loop(1, nchan, hello_group, 0)

    PR[0] = jnp.zeros(PR.shape[1:], BF16)
    PR[nchan + 1] = jnp.zeros(PR.shape[1:], BF16)
    WP[:, :, 192:256, :] = jnp.zeros((3, 3, 64, WP.shape[3]), BF16)
    T[:, :, 24:32, :] = jnp.zeros((2, nchip, 8, 128), F32)
    l_fe.wait()
    F3[:, 1:3] = along_z(FE[:, 1:3].reshape(256, 128).astype(F32)).reshape(8, 2, 16, 384)
    l_go.wait()
    tap_sums((1,), (1,), feat_rows((1,)))

    pl.semaphore_wait(barrier, (nchan - 1) + (ny - 1) + (ZHI - 1) + 2)

    upper, lower = lax.rem(g + 1, ngrp), lax.rem(g + ngrp - 1, ngrp)
    right, left = group_of(1), group_of(nchan - 1)
    remote(FE.at[:, 2:3], FE.at[:, 0:1], es, er, g, right).start()
    remote(FE.at[:, 1:2], FE.at[:, 3:4], es, er, g, left).start()
    remote(G.at[10:11, 1:3], G.at[2:3, 1:3], ns, nr, upper, c).start()
    remote(G.at[3:4, 1:3], G.at[11:12, 1:3], ns, nr, lower, c).start()
    remote(G.at[8:10, 1:3], G.at[0:2, 1:3], qs, qr, upper, c).start()
    remote(G.at[4:6, 1:3], G.at[12:14, 1:3], qs, qr, lower, c).start()
    remote(G.at[3:11, 2:3], G.at[3:11, 0:1], rs, rr, g, right).start()
    remote(G.at[3:11, 1:2], G.at[3:11, 3:4], rs, rr, g, left).start()
    for s in range(1, ZHI):
        pl.semaphore_signal(ready, inc=1, device_id=dev(zgrp(s), c), device_id_type=MESH)
    to_partner(0)
    to_owners(0)
    arrived(FE.at[:, 1:3], er)
    for row, edge in ((0, 0), (3, nchan - 1)):
        shifted = along_z(FE[:, row:row + 1].reshape(128, 128).astype(F32)).reshape(8, 1, 16, 384)
        F3[:, row:row + 1] = jnp.where(c == edge, jnp.zeros_like(shifted), shifted)

    tap_sums((1,), (0, 2), feat_rows((0, 2)))
    to_partner(1)
    arrived(G.at[0:1, 0:4], nr)
    tap_sums((0, 2), (0, 1, 2), feat_rows((0, 1, 2)))
    to_partner(2)
    arrived(G.at[0:2, 0:4], qr)
    for planes in ((0, 3), (11, 14)):
        at = slice(planes[0], planes[1])
        remote(G.at[at, 2:3], G.at[at, 0:1], rs, rr, g, right).start()
        remote(G.at[at, 1:2], G.at[at, 3:4], rs, rr, g, left).start()
    to_owners(1)
    for t in range(3):
        l_wh[t].wait()
        remote(own_rows[t], own_rows[t], ws, wr, g, other).start()
    to_owners(2)
    l_wf.wait()
    l_up.wait()
    sent(G.at[0:7, 0:4], rs)
    arrived(G.at[0:7, 0:4], rr)

    @pl.when(g == 0)
    def _():
        G[0:3] = jnp.zeros((3,) + G.shape[1:], BF16)

    @pl.when(g == ngrp - 1)
    def _():
        G[11:14] = jnp.zeros((3,) + G.shape[1:], BF16)

    @pl.when(c == 0)
    def _():
        G[:, 0:1] = jnp.zeros((14, 1, 16, 128), BF16)

    @pl.when(c == nchan - 1)
    def _():
        G[:, 3:4] = jnp.zeros((14, 1, 16, 128), BF16)

    lhs = jnp.concatenate(
        [
            G[2 - tx:14 - tx, 2 - ty:4 - ty].reshape(384, 128)
            for tx in range(3)
            for ty in range(3)
        ],
        axis=1,
    )
    rhs = jnp.concatenate(
        [WF[tx, ty].reshape(384, 128) for tx in range(3) for ty in range(3)], axis=1
    )
    grown = lax.dot_general(lhs, rhs, NT, preferred_element_type=F32)
    z_at = lax.broadcasted_iota(jnp.int32, (384, 128), 0) % 16
    up = jnp.where(z_at < 15, pltpu.roll(grown[:, 0:128], 383, 0), 0.0)
    down = jnp.where(z_at > 0, pltpu.roll(grown[:, 256:384], 1, 0), 0.0)
    IG[...] = grown[:, 128:256] + up + down

    coarse = jnp.zeros((48, 512), F32)
    for a in range(2):
        for b in range(2):
            cells = jnp.concatenate(
                [
                    jnp.concatenate(
                        [IG[pl.ds(((2 * i + a) * 2 + b) * 16 + k, 8, stride=2), :] for i in range(6)],
                        axis=0,
                    )
                    for k in range(2)
                ],
                axis=1,
            ).astype(BF16)
            weight = jnp.concatenate([UP[a, b, 0], UP[a, b, 1]], axis=1)
            coarse = coarse + lax.dot_general(cells, weight, NT, preferred_element_type=F32)
    row_of = lax.broadcasted_iota(jnp.int32, (48, 512), 0)
    outside = ((row_of < 8) & (g == 0)) | ((row_of >= 40) & (g == ngrp - 1))
    coarse = jnp.where(outside, 0.0, coarse)
    low = lax.broadcasted_iota(jnp.int32, (8, 128), 1) < 64
    for q in range(4):
        block = coarse[:, q * 128:(q + 1) * 128]
        turned = pltpu.roll(block, 64, 1)
        for half in range(2):
            same, swap = (block, turned) if half == 0 else (turned, block)
            d = 2 * q + half
            for k in range(2):
                at = [coarse_row * 8 for coarse_row in range(2 * k, 2 * k + 4)]
                pair = [
                    jnp.where(low, same[at[r]:at[r] + 8], swap[at[r + 1]:at[r + 1] + 8]) for r in (0, 2)
                ]
                PS[2 * d + k] = jnp.concatenate(pair, axis=0).astype(BF16)

    for d in far_members:
        remote(PS.at[d], PR.at[c + 1], ps, pr, g, d).start()
    PR[c + 1] = PS[c]
    sums = []
    for part in range(3):
        arrived(SR.at[0:7, TAP_PART[part]], sr.at[part])
        total = T[core, chip, TAP_PART[part], :]
        for s in range(1, nchan // 2):
            total = total + SR[lax.rem(chip + s, nchip), TAP_PART[part], :].astype(F32)
        sums.append(total)
    flipped = jnp.concatenate(sums + [jnp.zeros((32, 128), F32)], axis=0).T
    top = lax.broadcasted_iota(jnp.int32, (8, 128), 0) < 4
    for r in range(16):
        left_half, right_half = flipped[8 * r:8 * r + 8, 0:128], flipped[8 * r:8 * r + 8, 128:256]
        YS[2 * r] = jnp.where(top, left_half, pltpu.roll(right_half, 4, 0)).astype(BF16)
        YS[2 * r + 1] = jnp.where(top, pltpu.roll(left_half, 4, 0), right_half).astype(BF16)
    pl.semaphore_wait(ready, ZHI - 1)
    for dy, dz in FAR_GROUPS:
        to = lax.rem(y + dy, ny) * ZHI + lax.rem(zh + dz, ZHI)
        remote(YS.at[to], YR.at[g], ys, yr, to, c).start()
    YR[g] = YS[g]

    arrived(WP.at[:, :, 0:96, :], wr)
    arrived(PR.at[0:15], pr)
    rows = (nchan + 2) * 8
    slab = PR[...].astype(F32)
    slab = jnp.concatenate([slab[:, 0:8, :], slab[:, 8:16, :]], axis=2).reshape(rows, 256)
    k_of = lax.broadcasted_iota(jnp.int32, (rows, 256), 0) % 8
    shifted = (
        jnp.where(k_of < 7, pltpu.roll(slab, rows - 1, 0), 0.0),
        slab,
        jnp.where(k_of > 0, pltpu.roll(slab, 1, 0), 0.0),
    )
    for tz in range(3):
        pair = [v.reshape(nchan + 2, 8, 256) for v in (shifted[tz], pltpu.roll(shifted[tz], 192, 1))]
        SA[tz] = jnp.concatenate(pair, axis=1).astype(BF16)
    lhs = jnp.concatenate(
        [
            SA[tz, 2 - ty:2 - ty + nchan].reshape(nchan * 16, 256)
            for ty in range(3)
            for tz in range(3)
        ],
        axis=1,
    )
    part = jnp.dot(lhs, WP[...].reshape(9 * 256, 512), preferred_element_type=F32)
    FS[...] = part.astype(BF16).reshape(FS.shape)

    for d in far_members:
        remote(FS.at[d], FR.at[c], fs, fr, g, d).start()
    FR[c] = FS[c]

    arrived(FR.at[0:15], fr)
    for k in range(2):
        acc = FR[k].astype(F32)
        for p in range(1, nchan // 2):
            acc = acc + FR[2 * p + k].astype(F32)
        gh_out[k * 16:(k + 1) * 16, :] = acc.astype(BF16)

    sent(FE.at[:, 1:3], es)
    sent(G.at[0:1, 0:4], ns)
    sent(G.at[0:2, 0:4], qs)
    sent(WP.at[:, :, 0:96, :], ws)
    for part in range(3):
        sent(XS.at[:, TAP_PART[part], :], xs.at[part])
        sent(SS.at[0:7, TAP_PART[part]], ss.at[part])
    sent(PS.at[0:15], ps)
    sent(FS.at[0:15], fs)
    sent(YS.at[0:31], ys)

    arrived(YR.at[0:31], yr)
    v3 = YR[0].astype(F32)
    for o in range(1, 32):
        v3 = v3 + YR[o].astype(F32)
    for tx in range(3):
        for ty in range(3):
            for tz in range(3):
                at = TAP_ROW[tx, ty] + tz * 8
                row, lane = at // 128 * 4, at % 128
                tg_out[(tx * 3 + ty) * 3 + tz] = v3[row:row + 4, lane:lane + 8]


def body(grad_out, feat_full, filters_full, upsample_weight, filters_half):
    nchan = lax.axis_size("chan")
    nchip = nchan // 2
    wide = filters_half.shape[3]
    turned = jnp.swapaxes(filters_half, 3, 4)
    V = pltpu.VMEM
    D = pltpu.SemaphoreType.DMA
    anyspace = pl.BlockSpec(memory_space=pl.ANY)
    vmem = pl.BlockSpec(memory_space=pltpu.VMEM)
    grad_half, taps = pl.pallas_call(
        kernel,
        out_shape=(
            pltpu.VMEM((32, wide), BF16),
            pltpu.VMEM((27, 4, 8), F32),
        ),
        in_specs=[anyspace] * 5,
        out_specs=(vmem, vmem),
        scratch_shapes=[
            V((14, 4, 16, 128), BF16),
            V((8, 4, 16, 128), BF16),
            V((8, 4, 16, 384), BF16),
            V((3, 3, 3, 128, 128), BF16),
            V((2, 2, 2, wide, 128), BF16),
            V((3, 3, 256, wide), BF16),
            V((384, 128), F32),
            V((2, nchip, 224, 128), F32),
            V((nchip, 224, 128), BF16),
            V((nchip, 224, 128), BF16),
            V((nchip, 224, 128), BF16),
            V((nchip, 224, 128), BF16),
            V((nchan, 16, 128), BF16),
            V((nchan + 2, 16, 128), BF16),
            V((3, nchan + 2, 16, 256), BF16),
            V((nchan, 16, wide), BF16),
            V((nchan, 16, wide), BF16),
            V((32, 8, 128), BF16),
            V((32, 8, 128), BF16),
            D((7,)),
            D, D, D, D, D, D, D, D, D, D,
            D((3,)), D((3,)), D((3,)), D((3,)),
            D, D, D, D, D, D, pltpu.SemaphoreType.REGULAR,
        ],
        compiler_params=pltpu.CompilerParams(collective_id=0, has_side_effects=True),
    )(grad_out, feat_full, filters_full, upsample_weight, turned)
    return grad_half.reshape(1, 4, 8, wide), taps.reshape(3, 3, 3, 4, 8)


def solution(mesh):
    in_specs = (
        P("grp", "chan", None, None),
        P("grp", "chan", None, None),
        P(),
        P(),
        P(None, None, None, None, "chan"),
    )
    out_specs = (P("chan", "grp", None, None), P(None, None, None, "grp", "chan"))
    return jax.shard_map(body, mesh=mesh, in_specs=in_specs, out_specs=out_specs, check_vma=False)
```

```python
import jax
import jax.numpy as jnp
from jax import lax
from jax.experimental import pallas as pl
from jax.experimental.pallas import tpu as pltpu
from jax.sharding import PartitionSpec as P

ZHI = 4
TAP_ROW = {
    (tx, ty): {1: {1: 0, 0: 32, 2: 56}, 0: {0: 80, 1: 104, 2: 128}, 2: {0: 152, 1: 176, 2: 200}}[tx][ty]
    for tx in range(3)
    for ty in range(3)
}
TAP_PART = (slice(0, 32), slice(32, 80), slice(80, 224))
FAR_CHIPS = ((1, 2), (0, 2), (1, 1), (1, 3), (0, 1), (0, 3), (1, 0))
FAR_GROUPS = sorted(
    ((dy, dz) for dy in range(8) for dz in range(ZHI) if dy + dz > 0),
    key=lambda d: -(min(d[0], 8 - d[0]) + 2 * min(d[1], ZHI - d[1])),
)
F32 = jnp.float32
BF16 = jnp.bfloat16
MESH = pl.DeviceIdType.MESH
NT = (((1,), (1,)), ((), ()))
TN = (((0,), (0,)), ((), ()))


def kernel(
    go, fe, wf, uw, wh,
    gh_out, tg_out,
    G, FE, F3, WF, UP, WP, IG,
    T, XS, XR, SS, SR,
    PS, PR, SA, FS, FR,
    YS, YR,
    lsem, es, er, ns, nr, qs, qr, bs, br, rs, rr, ws, wr, xs, xr, ss, sr, ps, pr, fs, fr, ys, yr, ready,
):
    g = lax.axis_index("grp")
    c = lax.axis_index("chan")
    ngrp = lax.axis_size("grp")
    nchan = lax.axis_size("chan")
    nchip = nchan // 2
    ny = ngrp // ZHI
    y, zh = g // ZHI, lax.rem(g, ZHI)
    chip, core = c // 2, lax.rem(c, 2)

    def dev(gi, ci):
        return {"grp": gi, "chan": ci}

    def remote(src, dst, send, recv, gi, ci):
        return pltpu.make_async_remote_copy(
            src_ref=src, dst_ref=dst, send_sem=send, recv_sem=recv,
            device_id=dev(gi, ci), device_id_type=MESH,
        )

    other = c + 1 - 2 * core

    def group_of(s):
        return lax.rem(c + s, nchan)

    def ygrp(s):
        return lax.rem(y + s, ny) * ZHI + zh

    def zgrp(s):
        return y * ZHI + lax.rem(zh + s, ZHI)

    def sent(ref, sem):
        remote(ref, ref, sem, sem, g, other).wait_send()

    def arrived(ref, sem):
        remote(ref, ref, sem, sem, g, other).wait_recv()

    def chip_at(dz, dx):
        return (chip // 4 + dz) % 2 * 4 + (chip % 4 + dx) % 4

    far_chips = [chip_at(dz, dx) for dz, dx in FAR_CHIPS]
    far_members = [2 * p + k for p in far_chips for k in range(2)] + [other]

    def tap_sums(txs, tys, feat3):
        planes = []
        for tx in txs:
            if tx == 0:
                last = jnp.where(g == ngrp - 1, jnp.zeros((1, 2, 16, 128), BF16), G[11:12, 1:3])
                window = jnp.concatenate([G[4:11, 1:3], last], axis=0)
            elif tx == 1:
                window = G[3:11, 1:3]
            else:
                first = jnp.where(g == 0, jnp.zeros((1, 2, 16, 128), BF16), G[2:3, 1:3])
                window = jnp.concatenate([first, G[3:10, 1:3]], axis=0)
            planes.append(window.reshape(256, 128))
        part = lax.dot_general(
            jnp.concatenate(planes, axis=1), feat3, TN, preferred_element_type=F32
        )
        for n, tx in enumerate(txs):
            rows = part[n * 128:(n + 1) * 128].reshape(nchip, 2, 8, feat3.shape[1])
            for m, ty in enumerate(tys):
                for tz in range(3):
                    at = TAP_ROW[tx, ty] + tz * 8
                    t = (m * 3 + tz) * 128
                    for k in range(2):
                        T[k, :, at:at + 8, :] = rows[:, k, :, t:t + 128]

    def to_partner(part):
        rows = TAP_PART[part]
        XS[:, rows, :] = T[1 - core, :, rows, :].astype(BF16)
        remote(XS.at[:, rows, :], XR.at[:, rows, :], xs.at[part], xr.at[part], g, other).start()

    def to_owners(part):
        rows = TAP_PART[part]
        arrived(XR.at[:, rows, :], xr.at[part])
        summed = T[core, :, rows, :] + XR[:, rows, :].astype(F32)
        T[core, :, rows, :] = summed
        SS[:, rows, :] = summed.astype(BF16)
        for d in far_chips:
            remote(
                SS.at[d, rows], SR.at[chip, rows], ss.at[part], sr.at[part], g, 2 * d + core
            ).start()

    def feat_rows(tys):
        return jnp.concatenate([F3[:, ty:ty + 2].reshape(256, 384) for ty in tys], axis=1)

    def along_z(cells):
        z_of = lax.broadcasted_iota(jnp.int32, cells.shape, 0) % 16
        before = jnp.where(z_of > 0, pltpu.roll(cells, 1, 0), 0.0)
        after = jnp.where(z_of < 15, pltpu.roll(cells, cells.shape[0] - 1, 0), 0.0)
        return jnp.concatenate([before, cells, after], axis=1).astype(BF16)

    l_go = pltpu.make_async_copy(go, G.at[3:11, 1:3], lsem.at[0])
    l_fe = pltpu.make_async_copy(fe, FE.at[:, 1:3], lsem.at[1])
    own_rows = [WP.at[:, :, pl.ds(pl.multiple_of((2 - t) * 64 + core * 32, 32), 32), :] for t in range(3)]
    l_wh = [pltpu.make_async_copy(wh.at[t], own_rows[t], lsem.at[2 + t]) for t in range(3)]
    l_wf = pltpu.make_async_copy(wf, WF, lsem.at[5])
    l_up = pltpu.make_async_copy(uw, UP, lsem.at[6])
    l_fe.start()
    l_go.start()
    for t in range(3):
        l_wh[t].start()
    l_wf.start()
    l_up.start()

    barrier = pltpu.get_barrier_semaphore()

    def hello(gi, ci):
        pl.semaphore_signal(barrier, inc=1, device_id=dev(gi, ci), device_id_type=MESH)

    def hello_group(s, _):
        hello(g, group_of(s))
        return 0

    def hello_y(s, _):
        hello(ygrp(s), c)
        return 0

    def hello_z(s, _):
        hello(zgrp(s), c)
        return 0

    for dg in (1, ngrp - 1):
        hello(lax.rem(g + dg, ngrp), c)
    lax.fori_loop(1, ny, hello_y, 0)
    lax.fori_loop(1, ZHI, hello_z, 0)
    lax.fori_loop(1, nchan, hello_group, 0)

    PR[0] = jnp.zeros(PR.shape[1:], BF16)
    PR[nchan + 1] = jnp.zeros(PR.shape[1:], BF16)
    WP[:, :, 192:256, :] = jnp.zeros((3, 3, 64, WP.shape[3]), BF16)
    T[:, :, 24:32, :] = jnp.zeros((2, nchip, 8, 128), F32)
    l_fe.wait()
    F3[:, 1:3] = along_z(FE[:, 1:3].reshape(256, 128).astype(F32)).reshape(8, 2, 16, 384)
    l_go.wait()
    tap_sums((1,), (1,), feat_rows((1,)))

    pl.semaphore_wait(barrier, (nchan - 1) + (ny - 1) + (ZHI - 1) + 2)

    upper, lower = lax.rem(g + 1, ngrp), lax.rem(g + ngrp - 1, ngrp)
    right, left = group_of(1), group_of(nchan - 1)
    remote(FE.at[:, 2:3], FE.at[:, 0:1], es, er, g, right).start()
    remote(FE.at[:, 1:2], FE.at[:, 3:4], es, er, g, left).start()
    remote(G.at[10:11, 1:3], G.at[2:3, 1:3], ns, nr, upper, c).start()
    remote(G.at[3:4, 1:3], G.at[11:12, 1:3], ns, nr, lower, c).start()
    remote(G.at[8:10, 1:3], G.at[0:2, 1:3], qs, qr, upper, c).start()
    remote(G.at[4:6, 1:3], G.at[12:14, 1:3], qs, qr, lower, c).start()
    remote(G.at[3:11, 2:3], G.at[3:11, 0:1], bs, br, g, right).start()
    remote(G.at[3:11, 1:2], G.at[3:11, 3:4], bs, br, g, left).start()
    for s in range(1, ZHI):
        pl.semaphore_signal(ready, inc=1, device_id=dev(zgrp(s), c), device_id_type=MESH)
    to_partner(0)
    to_owners(0)
    arrived(FE.at[:, 1:3], er)
    for row, edge in ((0, 0), (3, nchan - 1)):
        shifted = along_z(FE[:, row:row + 1].reshape(128, 128).astype(F32)).reshape(8, 1, 16, 384)
        F3[:, row:row + 1] = jnp.where(c == edge, jnp.zeros_like(shifted), shifted)

    tap_sums((1,), (0, 2), feat_rows((0, 2)))
    to_partner(1)
    arrived(G.at[0:1, 0:4], nr)
    arrived(G.at[0:2, 0:4], qr)
    for planes in ((0, 3), (11, 14)):
        at = slice(planes[0], planes[1])
        remote(G.at[at, 2:3], G.at[at, 0:1], rs, rr, g, right).start()
        remote(G.at[at, 1:2], G.at[at, 3:4], rs, rr, g, left).start()
    tap_sums((0, 2), (0, 1, 2), feat_rows((0, 1, 2)))
    to_partner(2)
    to_owners(1)
    for t in range(3):
        l_wh[t].wait()
        remote(own_rows[t], own_rows[t], ws, wr, g, other).start()
    to_owners(2)
    l_wf.wait()
    l_up.wait()
    arrived(G.at[0:4, 0:4], br)

    @pl.when(c == 0)
    def _():
        G[3:11, 0:1] = jnp.zeros((8, 1, 16, 128), BF16)

    @pl.when(c == nchan - 1)
    def _():
        G[3:11, 3:4] = jnp.zeros((8, 1, 16, 128), BF16)

    def gradient(starts, count, places):
        lhs = jnp.concatenate(
            [
                jnp.concatenate(
                    [G[s - tx:s - tx + count, 2 - ty:4 - ty].reshape(count * 32, 128) for s in starts],
                    axis=0,
                )
                for tx in range(3)
                for ty in range(3)
            ],
            axis=1,
        )
        rhs = jnp.concatenate(
            [WF[tx, ty].reshape(384, 128) for tx in range(3) for ty in range(3)], axis=1
        )
        grown = lax.dot_general(lhs, rhs, NT, preferred_element_type=F32)
        z_at = lax.broadcasted_iota(jnp.int32, (192, 128), 0) % 16
        up = jnp.where(z_at < 15, pltpu.roll(grown[:, 0:128], 191, 0), 0.0)
        down = jnp.where(z_at > 0, pltpu.roll(grown[:, 256:384], 1, 0), 0.0)
        whole = grown[:, 128:256] + up + down
        for n, place in enumerate(places):
            IG[place:place + count * 32, :] = whole[n * count * 32:(n + 1) * count * 32]

    gradient((5,), 6, (96,))
    sent(G.at[0:3, 0:4], rs)
    arrived(G.at[0:3, 0:4], rr)

    @pl.when(g == 0)
    def _():
        G[0:3] = jnp.zeros((3,) + G.shape[1:], BF16)

    @pl.when(g == ngrp - 1)
    def _():
        G[11:14] = jnp.zeros((3,) + G.shape[1:], BF16)

    @pl.when(c == 0)
    def _():
        G[:, 0:1] = jnp.zeros((14, 1, 16, 128), BF16)

    @pl.when(c == nchan - 1)
    def _():
        G[:, 3:4] = jnp.zeros((14, 1, 16, 128), BF16)

    gradient((2, 11), 3, (0, 288))

    coarse = jnp.zeros((48, 512), F32)
    for a in range(2):
        for b in range(2):
            cells = jnp.concatenate(
                [
                    jnp.concatenate(
                        [IG[pl.ds(((2 * i + a) * 2 + b) * 16 + k, 8, stride=2), :] for i in range(6)],
                        axis=0,
                    )
                    for k in range(2)
                ],
                axis=1,
            ).astype(BF16)
            weight = jnp.concatenate([UP[a, b, 0], UP[a, b, 1]], axis=1)
            coarse = coarse + lax.dot_general(cells, weight, NT, preferred_element_type=F32)
    row_of = lax.broadcasted_iota(jnp.int32, (48, 512), 0)
    outside = ((row_of < 8) & (g == 0)) | ((row_of >= 40) & (g == ngrp - 1))
    coarse = jnp.where(outside, 0.0, coarse)
    low = lax.broadcasted_iota(jnp.int32, (8, 128), 1) < 64
    for q in range(4):
        block = coarse[:, q * 128:(q + 1) * 128]
        turned = pltpu.roll(block, 64, 1)
        for half in range(2):
            same, swap = (block, turned) if half == 0 else (turned, block)
            d = 2 * q + half
            for k in range(2):
                at = [coarse_row * 8 for coarse_row in range(2 * k, 2 * k + 4)]
                pair = [
                    jnp.where(low, same[at[r]:at[r] + 8], swap[at[r + 1]:at[r + 1] + 8]) for r in (0, 2)
                ]
                PS[2 * d + k] = jnp.concatenate(pair, axis=0).astype(BF16)

    for d in far_members:
        remote(PS.at[d], PR.at[c + 1], ps, pr, g, d).start()
    PR[c + 1] = PS[c]
    sums = []
    for part in range(3):
        arrived(SR.at[0:7, TAP_PART[part]], sr.at[part])
        total = T[core, chip, TAP_PART[part], :]
        for s in range(1, nchan // 2):
            total = total + SR[lax.rem(chip + s, nchip), TAP_PART[part], :].astype(F32)
        sums.append(total)
    flipped = jnp.concatenate(sums + [jnp.zeros((32, 128), F32)], axis=0).T
    top = lax.broadcasted_iota(jnp.int32, (8, 128), 0) < 4
    for r in range(16):
        left_half, right_half = flipped[8 * r:8 * r + 8, 0:128], flipped[8 * r:8 * r + 8, 128:256]
        YS[2 * r] = jnp.where(top, left_half, pltpu.roll(right_half, 4, 0)).astype(BF16)
        YS[2 * r + 1] = jnp.where(top, pltpu.roll(left_half, 4, 0), right_half).astype(BF16)
    pl.semaphore_wait(ready, ZHI - 1)
    for dy, dz in FAR_GROUPS:
        to = lax.rem(y + dy, ny) * ZHI + lax.rem(zh + dz, ZHI)
        remote(YS.at[to], YR.at[g], ys, yr, to, c).start()
    YR[g] = YS[g]

    arrived(WP.at[:, :, 0:96, :], wr)
    arrived(PR.at[0:15], pr)
    rows = (nchan + 2) * 8
    slab = PR[...].astype(F32)
    slab = jnp.concatenate([slab[:, 0:8, :], slab[:, 8:16, :]], axis=2).reshape(rows, 256)
    k_of = lax.broadcasted_iota(jnp.int32, (rows, 256), 0) % 8
    shifted = (
        jnp.where(k_of < 7, pltpu.roll(slab, rows - 1, 0), 0.0),
        slab,
        jnp.where(k_of > 0, pltpu.roll(slab, 1, 0), 0.0),
    )
    for tz in range(3):
        pair = [v.reshape(nchan + 2, 8, 256) for v in (shifted[tz], pltpu.roll(shifted[tz], 192, 1))]
        SA[tz] = jnp.concatenate(pair, axis=1).astype(BF16)
    lhs = jnp.concatenate(
        [
            SA[tz, 2 - ty:2 - ty + nchan].reshape(nchan * 16, 256)
            for ty in range(3)
            for tz in range(3)
        ],
        axis=1,
    )
    for half in range(2):
        cols = slice(half * 256, half * 256 + 256)
        part = jnp.dot(lhs, WP[:, :, :, cols].reshape(9 * 256, 256), preferred_element_type=F32)
        FS[:, :, cols] = part.astype(BF16).reshape(nchan, 16, 256)
        for d in far_members:
            remote(FS.at[d, :, cols], FR.at[c, :, cols], fs, fr, g, d).start()
    FR[c] = FS[c]

    arrived(FR.at[0:15], fr)
    for k in range(2):
        acc = FR[k].astype(F32)
        for p in range(1, nchan // 2):
            acc = acc + FR[2 * p + k].astype(F32)
        gh_out[k * 16:(k + 1) * 16, :] = acc.astype(BF16)

    sent(FE.at[:, 1:3], es)
    sent(G.at[0:1, 0:4], ns)
    sent(G.at[0:2, 0:4], qs)
    sent(G.at[0:4, 0:4], bs)
    sent(WP.at[:, :, 0:96, :], ws)
    for part in range(3):
        sent(XS.at[:, TAP_PART[part], :], xs.at[part])
        sent(SS.at[0:7, TAP_PART[part]], ss.at[part])
    sent(PS.at[0:15], ps)
    sent(FS.at[0:15], fs)
    sent(YS.at[0:31], ys)

    arrived(YR.at[0:31], yr)
    v3 = YR[0].astype(F32)
    for o in range(1, 32):
        v3 = v3 + YR[o].astype(F32)
    for tx in range(3):
        for ty in range(3):
            for tz in range(3):
                at = TAP_ROW[tx, ty] + tz * 8
                row, lane = at // 128 * 4, at % 128
                tg_out[(tx * 3 + ty) * 3 + tz] = v3[row:row + 4, lane:lane + 8]


def body(grad_out, feat_full, filters_full, upsample_weight, filters_half):
    nchan = lax.axis_size("chan")
    nchip = nchan // 2
    wide = filters_half.shape[3]
    turned = jnp.swapaxes(filters_half, 3, 4)
    V = pltpu.VMEM
    D = pltpu.SemaphoreType.DMA
    anyspace = pl.BlockSpec(memory_space=pl.ANY)
    vmem = pl.BlockSpec(memory_space=pltpu.VMEM)
    grad_half, taps = pl.pallas_call(
        kernel,
        out_shape=(
            pltpu.VMEM((32, wide), BF16),
            pltpu.VMEM((27, 4, 8), F32),
        ),
        in_specs=[anyspace] * 5,
        out_specs=(vmem, vmem),
        scratch_shapes=[
            V((14, 4, 16, 128), BF16),
            V((8, 4, 16, 128), BF16),
            V((8, 4, 16, 384), BF16),
            V((3, 3, 3, 128, 128), BF16),
            V((2, 2, 2, wide, 128), BF16),
            V((3, 3, 256, wide), BF16),
            V((384, 128), F32),
            V((2, nchip, 224, 128), F32),
            V((nchip, 224, 128), BF16),
            V((nchip, 224, 128), BF16),
            V((nchip, 224, 128), BF16),
            V((nchip, 224, 128), BF16),
            V((nchan, 16, 128), BF16),
            V((nchan + 2, 16, 128), BF16),
            V((3, nchan + 2, 16, 256), BF16),
            V((nchan, 16, wide), BF16),
            V((nchan, 16, wide), BF16),
            V((32, 8, 128), BF16),
            V((32, 8, 128), BF16),
            D((7,)),
            D, D, D, D, D, D, D, D, D, D, D, D,
            D((3,)), D((3,)), D((3,)), D((3,)),
            D, D, D, D, D, D, pltpu.SemaphoreType.REGULAR,
        ],
        compiler_params=pltpu.CompilerParams(collective_id=0, has_side_effects=True),
    )(grad_out, feat_full, filters_full, upsample_weight, turned)
    return grad_half.reshape(1, 4, 8, wide), taps.reshape(3, 3, 3, 4, 8)


def solution(mesh):
    in_specs = (
        P("grp", "chan", None, None),
        P("grp", "chan", None, None),
        P(),
        P(),
        P(None, None, None, None, "chan"),
    )
    out_specs = (P("chan", "grp", None, None), P(None, None, None, "grp", "chan"))
    return jax.shard_map(body, mesh=mesh, in_specs=in_specs, out_specs=out_specs, check_vma=False)
```

```python
import jax
import jax.numpy as jnp
from jax import lax
from jax.experimental import pallas as pl
from jax.experimental.pallas import tpu as pltpu
from jax.sharding import PartitionSpec as P

ZHI = 4
TAP_ROW = {
    (tx, ty): {1: {1: 0, 0: 32, 2: 56}, 0: {0: 80, 1: 104, 2: 128}, 2: {0: 152, 1: 176, 2: 200}}[tx][ty]
    for tx in range(3)
    for ty in range(3)
}
TAP_PART = (slice(0, 32), slice(32, 80), slice(80, 224))
FAR_CHIPS = ((1, 2), (0, 2), (1, 1), (1, 3), (0, 1), (0, 3), (1, 0))
FAR_GROUPS = sorted(
    ((dy, dz) for dy in range(8) for dz in range(ZHI) if dy + dz > 0),
    key=lambda d: -(min(d[0], 8 - d[0]) + 2 * min(d[1], ZHI - d[1])),
)
F32 = jnp.float32
BF16 = jnp.bfloat16
MESH = pl.DeviceIdType.MESH
NT = (((1,), (1,)), ((), ()))
TN = (((0,), (0,)), ((), ()))


def kernel(
    go, fe, wf, uw, wh,
    gh_out, tg_out,
    G, FE, F3, WF, UP, WP, IG,
    T, XS, XR, SS, SR,
    PS, PR, SA, FS, FR,
    YS, YR,
    lsem, es, er, ns, nr, qs, qr, bs, br, rs, rr, ws, wr, xs, xr, ss, sr, ps, pr, fs, fr, ys, yr, ready,
):
    g = lax.axis_index("grp")
    c = lax.axis_index("chan")
    ngrp = lax.axis_size("grp")
    nchan = lax.axis_size("chan")
    nchip = nchan // 2
    ny = ngrp // ZHI
    y, zh = g // ZHI, lax.rem(g, ZHI)
    chip, core = c // 2, lax.rem(c, 2)

    def dev(gi, ci):
        return {"grp": gi, "chan": ci}

    def remote(src, dst, send, recv, gi, ci):
        return pltpu.make_async_remote_copy(
            src_ref=src, dst_ref=dst, send_sem=send, recv_sem=recv,
            device_id=dev(gi, ci), device_id_type=MESH,
        )

    other = c + 1 - 2 * core

    def group_of(s):
        return lax.rem(c + s, nchan)

    def ygrp(s):
        return lax.rem(y + s, ny) * ZHI + zh

    def zgrp(s):
        return y * ZHI + lax.rem(zh + s, ZHI)

    def sent(ref, sem):
        remote(ref, ref, sem, sem, g, other).wait_send()

    def arrived(ref, sem):
        remote(ref, ref, sem, sem, g, other).wait_recv()

    def chip_at(dz, dx):
        return (chip // 4 + dz) % 2 * 4 + (chip % 4 + dx) % 4

    far_chips = [chip_at(dz, dx) for dz, dx in FAR_CHIPS]
    far_members = [
        (2 * p + k, dz) for p, (dz, _) in zip(far_chips, FAR_CHIPS) for k in range(2)
    ] + [(other, 0)]
    near_side, far_side = c // 8 * 8, 8 - c // 8 * 8

    def tap_sums(txs, tys, feat3):
        planes = []
        for tx in txs:
            if tx == 0:
                last = jnp.where(g == ngrp - 1, jnp.zeros((1, 2, 16, 128), BF16), G[11:12, 1:3])
                window = jnp.concatenate([G[4:11, 1:3], last], axis=0)
            elif tx == 1:
                window = G[3:11, 1:3]
            else:
                first = jnp.where(g == 0, jnp.zeros((1, 2, 16, 128), BF16), G[2:3, 1:3])
                window = jnp.concatenate([first, G[3:10, 1:3]], axis=0)
            planes.append(window.reshape(256, 128))
        part = lax.dot_general(
            jnp.concatenate(planes, axis=1), feat3, TN, preferred_element_type=F32
        )
        for n, tx in enumerate(txs):
            rows = part[n * 128:(n + 1) * 128].reshape(nchip, 2, 8, feat3.shape[1])
            for m, ty in enumerate(tys):
                for tz in range(3):
                    at = TAP_ROW[tx, ty] + tz * 8
                    t = (m * 3 + tz) * 128
                    for k in range(2):
                        T[k, :, at:at + 8, :] = rows[:, k, :, t:t + 128]

    def to_partner(part):
        rows = TAP_PART[part]
        XS[:, rows, :] = T[1 - core, :, rows, :].astype(BF16)
        remote(XS.at[:, rows, :], XR.at[:, rows, :], xs.at[part], xr.at[part], g, other).start()

    def to_owners(part):
        rows = TAP_PART[part]
        arrived(XR.at[:, rows, :], xr.at[part])
        summed = T[core, :, rows, :] + XR[:, rows, :].astype(F32)
        T[core, :, rows, :] = summed
        SS[:, rows, :] = summed.astype(BF16)
        for d in far_chips:
            remote(
                SS.at[d, rows], SR.at[chip, rows], ss.at[part], sr.at[part], g, 2 * d + core
            ).start()

    def feat_rows(tys):
        return jnp.concatenate([F3[:, ty:ty + 2].reshape(256, 384) for ty in tys], axis=1)

    def along_z(cells):
        z_of = lax.broadcasted_iota(jnp.int32, cells.shape, 0) % 16
        before = jnp.where(z_of > 0, pltpu.roll(cells, 1, 0), 0.0)
        after = jnp.where(z_of < 15, pltpu.roll(cells, cells.shape[0] - 1, 0), 0.0)
        return jnp.concatenate([before, cells, after], axis=1).astype(BF16)

    l_go = pltpu.make_async_copy(go, G.at[3:11, 1:3], lsem.at[0])
    l_fe = pltpu.make_async_copy(fe, FE.at[:, 1:3], lsem.at[1])
    own_rows = [WP.at[:, :, pl.ds(pl.multiple_of((2 - t) * 64 + core * 32, 32), 32), :] for t in range(3)]
    l_wh = [pltpu.make_async_copy(wh.at[t], own_rows[t], lsem.at[2 + t]) for t in range(3)]
    l_wf = pltpu.make_async_copy(wf, WF, lsem.at[5])
    l_up = pltpu.make_async_copy(uw, UP, lsem.at[6])
    l_fe.start()
    l_go.start()
    for t in range(3):
        l_wh[t].start()
    l_wf.start()
    l_up.start()

    barrier = pltpu.get_barrier_semaphore()

    def hello(gi, ci):
        pl.semaphore_signal(barrier, inc=1, device_id=dev(gi, ci), device_id_type=MESH)

    def hello_group(s, _):
        hello(g, group_of(s))
        return 0

    def hello_y(s, _):
        hello(ygrp(s), c)
        return 0

    def hello_z(s, _):
        hello(zgrp(s), c)
        return 0

    for dg in (1, ngrp - 1):
        hello(lax.rem(g + dg, ngrp), c)
    lax.fori_loop(1, ny, hello_y, 0)
    lax.fori_loop(1, ZHI, hello_z, 0)
    lax.fori_loop(1, nchan, hello_group, 0)

    for slot in (0, nchan + 1):
        SA[:, slot] = jnp.zeros((3, 16, 256), BF16)
    WP[:, :, 192:256, :] = jnp.zeros((3, 3, 64, WP.shape[3]), BF16)
    T[:, :, 24:32, :] = jnp.zeros((2, nchip, 8, 128), F32)
    l_fe.wait()
    F3[:, 1:3] = along_z(FE[:, 1:3].reshape(256, 128).astype(F32)).reshape(8, 2, 16, 384)
    l_go.wait()
    tap_sums((1,), (1,), feat_rows((1,)))

    pl.semaphore_wait(barrier, (nchan - 1) + (ny - 1) + (ZHI - 1) + 2)

    upper, lower = lax.rem(g + 1, ngrp), lax.rem(g + ngrp - 1, ngrp)
    right, left = group_of(1), group_of(nchan - 1)
    remote(FE.at[:, 2:3], FE.at[:, 0:1], es, er, g, right).start()
    remote(FE.at[:, 1:2], FE.at[:, 3:4], es, er, g, left).start()
    remote(G.at[10:11, 1:3], G.at[2:3, 1:3], ns, nr, upper, c).start()
    remote(G.at[3:4, 1:3], G.at[11:12, 1:3], ns, nr, lower, c).start()
    remote(G.at[8:10, 1:3], G.at[0:2, 1:3], qs, qr, upper, c).start()
    remote(G.at[4:6, 1:3], G.at[12:14, 1:3], qs, qr, lower, c).start()
    remote(G.at[3:11, 2:3], G.at[3:11, 0:1], bs, br, g, right).start()
    remote(G.at[3:11, 1:2], G.at[3:11, 3:4], bs, br, g, left).start()
    for s in range(1, ZHI):
        pl.semaphore_signal(ready, inc=1, device_id=dev(zgrp(s), c), device_id_type=MESH)
    to_partner(0)
    to_owners(0)
    arrived(FE.at[:, 1:3], er)
    for row, edge in ((0, 0), (3, nchan - 1)):
        shifted = along_z(FE[:, row:row + 1].reshape(128, 128).astype(F32)).reshape(8, 1, 16, 384)
        F3[:, row:row + 1] = jnp.where(c == edge, jnp.zeros_like(shifted), shifted)

    tap_sums((1,), (0, 2), feat_rows((0, 2)))
    to_partner(1)
    arrived(G.at[0:1, 0:4], nr)
    arrived(G.at[0:2, 0:4], qr)
    for planes in ((0, 3), (11, 14)):
        at = slice(planes[0], planes[1])
        remote(G.at[at, 2:3], G.at[at, 0:1], rs, rr, g, right).start()
        remote(G.at[at, 1:2], G.at[at, 3:4], rs, rr, g, left).start()
    tap_sums((0, 2), (0, 1, 2), feat_rows((0, 1, 2)))
    to_partner(2)
    to_owners(1)
    for t in range(3):
        l_wh[t].wait()
        remote(own_rows[t], own_rows[t], ws, wr, g, other).start()
    to_owners(2)
    l_wf.wait()
    l_up.wait()
    arrived(G.at[0:4, 0:4], br)

    @pl.when(c == 0)
    def _():
        G[3:11, 0:1] = jnp.zeros((8, 1, 16, 128), BF16)

    @pl.when(c == nchan - 1)
    def _():
        G[3:11, 3:4] = jnp.zeros((8, 1, 16, 128), BF16)

    def gradient(starts, count, places):
        lhs = jnp.concatenate(
            [
                jnp.concatenate(
                    [G[s - tx:s - tx + count, 2 - ty:4 - ty].reshape(count * 32, 128) for s in starts],
                    axis=0,
                )
                for tx in range(3)
                for ty in range(3)
            ],
            axis=1,
        )
        rhs = jnp.concatenate(
            [WF[tx, ty].reshape(384, 128) for tx in range(3) for ty in range(3)], axis=1
        )
        grown = lax.dot_general(lhs, rhs, NT, preferred_element_type=F32)
        z_at = lax.broadcasted_iota(jnp.int32, (192, 128), 0) % 16
        up = jnp.where(z_at < 15, pltpu.roll(grown[:, 0:128], 191, 0), 0.0)
        down = jnp.where(z_at > 0, pltpu.roll(grown[:, 256:384], 1, 0), 0.0)
        whole = grown[:, 128:256] + up + down
        for n, place in enumerate(places):
            IG[place:place + count * 32, :] = whole[n * count * 32:(n + 1) * count * 32]

    gradient((5,), 6, (96,))
    sent(G.at[0:3, 0:4], rs)
    arrived(G.at[0:3, 0:4], rr)

    @pl.when(g == 0)
    def _():
        G[0:3] = jnp.zeros((3,) + G.shape[1:], BF16)

    @pl.when(g == ngrp - 1)
    def _():
        G[11:14] = jnp.zeros((3,) + G.shape[1:], BF16)

    @pl.when(c == 0)
    def _():
        G[:, 0:1] = jnp.zeros((14, 1, 16, 128), BF16)

    @pl.when(c == nchan - 1)
    def _():
        G[:, 3:4] = jnp.zeros((14, 1, 16, 128), BF16)

    gradient((2, 11), 3, (0, 288))

    coarse = jnp.zeros((48, 512), F32)
    for a in range(2):
        for b in range(2):
            cells = jnp.concatenate(
                [
                    jnp.concatenate(
                        [IG[pl.ds(((2 * i + a) * 2 + b) * 16 + k, 8, stride=2), :] for i in range(6)],
                        axis=0,
                    )
                    for k in range(2)
                ],
                axis=1,
            ).astype(BF16)
            weight = jnp.concatenate([UP[a, b, 0], UP[a, b, 1]], axis=1)
            coarse = coarse + lax.dot_general(cells, weight, NT, preferred_element_type=F32)
    row_of = lax.broadcasted_iota(jnp.int32, (48, 512), 0)
    outside = ((row_of < 8) & (g == 0)) | ((row_of >= 40) & (g == ngrp - 1))
    coarse = jnp.where(outside, 0.0, coarse)
    low = lax.broadcasted_iota(jnp.int32, (8, 128), 1) < 64
    for q in range(4):
        block = coarse[:, q * 128:(q + 1) * 128]
        turned = pltpu.roll(block, 64, 1)
        for half in range(2):
            same, swap = (block, turned) if half == 0 else (turned, block)
            d = 2 * q + half
            for k in range(2):
                at = [coarse_row * 8 for coarse_row in range(2 * k, 2 * k + 4)]
                pair = [
                    jnp.where(low, same[at[r]:at[r] + 8], swap[at[r + 1]:at[r + 1] + 8]) for r in (0, 2)
                ]
                PS[2 * d + k] = jnp.concatenate(pair, axis=0).astype(BF16)

    for d, dz in far_members:
        remote(PS.at[d], PR.at[c + 1], ps, pr.at[dz], g, d).start()
    PR[c + 1] = PS[c]
    sums = []
    for part in range(3):
        arrived(SR.at[0:7, TAP_PART[part]], sr.at[part])
        total = T[core, chip, TAP_PART[part], :]
        for s in range(1, nchan // 2):
            total = total + SR[lax.rem(chip + s, nchip), TAP_PART[part], :].astype(F32)
        sums.append(total)
    flipped = jnp.concatenate(sums + [jnp.zeros((32, 128), F32)], axis=0).T
    top = lax.broadcasted_iota(jnp.int32, (8, 128), 0) < 4
    for r in range(16):
        left_half, right_half = flipped[8 * r:8 * r + 8, 0:128], flipped[8 * r:8 * r + 8, 128:256]
        YS[2 * r] = jnp.where(top, left_half, pltpu.roll(right_half, 4, 0)).astype(BF16)
        YS[2 * r + 1] = jnp.where(top, pltpu.roll(left_half, 4, 0), right_half).astype(BF16)
    pl.semaphore_wait(ready, ZHI - 1)
    for dy, dz in FAR_GROUPS:
        to = lax.rem(y + dy, ny) * ZHI + lax.rem(zh + dz, ZHI)
        remote(YS.at[to], YR.at[g], ys, yr, to, c).start()
    YR[g] = YS[g]

    arrived(WP.at[:, :, 0:96, :], wr)
    k_of = lax.broadcasted_iota(jnp.int32, (64, 256), 0) % 8
    for dz, count, side in ((0, 7, near_side), (1, 8, far_side)):
        arrived(PR.at[0:count], pr.at[dz])
        slots = pl.ds(1 + side, 8)
        slab = PR[slots].astype(F32)
        slab = jnp.concatenate([slab[:, 0:8, :], slab[:, 8:16, :]], axis=2).reshape(64, 256)
        shifted = (
            jnp.where(k_of < 7, pltpu.roll(slab, 63, 0), 0.0),
            slab,
            jnp.where(k_of > 0, pltpu.roll(slab, 1, 0), 0.0),
        )
        for tz in range(3):
            pair = [v.reshape(8, 8, 256) for v in (shifted[tz], pltpu.roll(shifted[tz], 192, 1))]
            SA[tz, slots] = jnp.concatenate(pair, axis=1).astype(BF16)
    lhs = jnp.concatenate(
        [
            SA[tz, 2 - ty:2 - ty + nchan].reshape(nchan * 16, 256)
            for ty in range(3)
            for tz in range(3)
        ],
        axis=1,
    )
    part = jnp.dot(lhs, WP[...].reshape(9 * 256, 512), preferred_element_type=F32)
    FS[...] = part.astype(BF16).reshape(FS.shape)
    for d, dz in far_members:
        remote(FS.at[d], FR.at[c], fs, fr.at[dz], g, d).start()
    FR[c] = FS[c]

    half_sums = [jnp.zeros((16, FR.shape[2]), F32)] * 2
    for dz, count, side in ((0, 7, near_side), (1, 8, far_side)):
        arrived(FR.at[0:count], fr.at[dz])
        for k in range(2):
            for p in range(4):
                half_sums[k] = half_sums[k] + FR[side + 2 * p + k].astype(F32)
    for k in range(2):
        gh_out[k * 16:(k + 1) * 16, :] = half_sums[k].astype(BF16)

    sent(FE.at[:, 1:3], es)
    sent(G.at[0:1, 0:4], ns)
    sent(G.at[0:2, 0:4], qs)
    sent(G.at[0:4, 0:4], bs)
    sent(WP.at[:, :, 0:96, :], ws)
    for part in range(3):
        sent(XS.at[:, TAP_PART[part], :], xs.at[part])
        sent(SS.at[0:7, TAP_PART[part]], ss.at[part])
    sent(PS.at[0:15], ps)
    sent(FS.at[0:15], fs)
    sent(YS.at[0:31], ys)

    arrived(YR.at[0:31], yr)
    v3 = YR[0].astype(F32)
    for o in range(1, 32):
        v3 = v3 + YR[o].astype(F32)
    for tx in range(3):
        for ty in range(3):
            for tz in range(3):
                at = TAP_ROW[tx, ty] + tz * 8
                row, lane = at // 128 * 4, at % 128
                tg_out[(tx * 3 + ty) * 3 + tz] = v3[row:row + 4, lane:lane + 8]


def finish(half_ref, taps_ref, half_out, taps_out, sem):
    copies = [
        pltpu.make_async_copy(half_ref, half_out, sem.at[0]),
        pltpu.make_async_copy(taps_ref, taps_out, sem.at[1]),
    ]
    for copy in copies:
        copy.start()
    for copy in copies:
        copy.wait()


def body(grad_out, feat_full, filters_full, upsample_weight, filters_half):
    nchan = lax.axis_size("chan")
    nchip = nchan // 2
    wide = filters_half.shape[3]
    turned = jnp.swapaxes(filters_half, 3, 4)
    V = pltpu.VMEM
    D = pltpu.SemaphoreType.DMA
    anyspace = pl.BlockSpec(memory_space=pl.ANY)
    vmem = pl.BlockSpec(memory_space=pltpu.VMEM)
    grad_half, taps = pl.pallas_call(
        kernel,
        out_shape=(
            pltpu.VMEM((32, wide), BF16),
            pltpu.VMEM((27, 4, 8), F32),
        ),
        in_specs=[anyspace] * 5,
        out_specs=(vmem, vmem),
        scratch_shapes=[
            V((14, 4, 16, 128), BF16),
            V((8, 4, 16, 128), BF16),
            V((8, 4, 16, 384), BF16),
            V((3, 3, 3, 128, 128), BF16),
            V((2, 2, 2, wide, 128), BF16),
            V((3, 3, 256, wide), BF16),
            V((384, 128), F32),
            V((2, nchip, 224, 128), F32),
            V((nchip, 224, 128), BF16),
            V((nchip, 224, 128), BF16),
            V((nchip, 224, 128), BF16),
            V((nchip, 224, 128), BF16),
            V((nchan, 16, 128), BF16),
            V((nchan + 2, 16, 128), BF16),
            V((3, nchan + 2, 16, 256), BF16),
            V((nchan, 16, wide), BF16),
            V((nchan, 16, wide), BF16),
            V((32, 8, 128), BF16),
            V((32, 8, 128), BF16),
            D((7,)),
            D, D, D, D, D, D, D, D, D, D, D, D,
            D((3,)), D((3,)), D((3,)), D((3,)),
            D, D((2,)), D, D((2,)), D, D, pltpu.SemaphoreType.REGULAR,
        ],
        compiler_params=pltpu.CompilerParams(collective_id=0, has_side_effects=True),
    )(grad_out, feat_full, filters_full, upsample_weight, turned)
    grad_half, taps = pl.pallas_call(
        finish,
        out_shape=(
            jax.ShapeDtypeStruct((32, wide), BF16),
            jax.ShapeDtypeStruct((27, 4, 8), F32),
        ),
        in_specs=[vmem, vmem],
        out_specs=(anyspace, anyspace),
        scratch_shapes=[D((2,))],
        compiler_params=pltpu.CompilerParams(vmem_limit_bytes=1 << 20),
    )(grad_half, taps)
    return grad_half.reshape(1, 4, 8, wide), taps.reshape(3, 3, 3, 4, 8)


def solution(mesh):
    in_specs = (
        P("grp", "chan", None, None),
        P("grp", "chan", None, None),
        P(),
        P(),
        P(None, None, None, None, "chan"),
    )
    out_specs = (P("chan", "grp", None, None), P(None, None, None, "grp", "chan"))
    return jax.shard_map(body, mesh=mesh, in_specs=in_specs, out_specs=out_specs, check_vma=False)
```
